256 devices in a mesh: seq: 32 (over y, z), head: 8 (over x, core).
Axes of the slice: x: 4, y: 4, z: 8, core: 2. Of those that a mesh axis runs over, the one named last changes fastest.
Arguments:
- query: bfloat16 [16384, 2048], P('seq', 'head'), may hold values from -6 to 6
- keys: bfloat16 [16384, 2048], P('seq', 'head'), may hold values from -6 to 6
- values: bfloat16 [16384, 4096], P('seq', 'head'), may hold values from -6 to 6
- gate_logit: float32 [16384, 32], P('seq', 'head'), may hold values from -17 to 1.5
- beta_logit: float32 [16384, 32], P('seq', 'head'), may hold values from -9 to 6
- decay_rate: float32 [32], P('head'), may hold values from 0.5 to 8
- norm_gain: float32 [128], replicated, may hold values from 0.1 to 1.9
- gate_z: bfloat16 [16384, 4096], P('seq', 'head'), may hold values from -6 to 6
- out_weight: bfloat16 [4096, 2048], P('head'), may hold values from -0.09375 to 0.09375
Outputs:
- mixed: bfloat16 [16384, 2048], P(('seq', 'head'))
The draws below stay inside these ranges and needn't reach their ends.
All inputs are finite; a program needn't handle non-finite values.
Results may differ from the reference program's by a relative error of at most 0.014.
Values may be sent and summed in bfloat16 or wider, within the bound.
A program may use at most 128 MiB of HBM per device.

```python
import math
import jax
import jax.numpy as jnp
from jax import lax

D = 2048
VALUE_HEADS = 32
DK = 128
DV = 128
SPAN = 64
HK = 16
SEQUENCE_TOKENS = 16384


def head_plan(key):
    chosen = jax.random.uniform(jax.random.fold_in(key, 101), (VALUE_HEADS,), jnp.float32)
    slow_heads = chosen < 0.5
    head_rates = jnp.exp(jax.random.uniform(jax.random.fold_in(key, 102), (VALUE_HEADS,), jnp.float32, math.log(0.5), math.log(8.0)))
    return (slow_heads, head_rates)


def jitter(key):
    return jnp.clip(0.6 * jax.random.normal(key, (SEQUENCE_TOKENS, VALUE_HEADS), jnp.float32), -1.5, 1.5)


def draw_decay_rate(key, part):
    slow_heads, head_rates = head_plan(key)
    return head_rates


def draw_gate_logit(key, part):
    slow_heads, head_rates = head_plan(key)
    spread_part = jitter(jax.random.fold_in(key, 103))
    phases = jax.random.uniform(jax.random.fold_in(key, 104), (VALUE_HEADS,), jnp.float32, 0.0, 2.0 * math.pi)
    position = jnp.arange(SEQUENCE_TOKENS, dtype=jnp.float32)[:, None] / SEQUENCE_TOKENS
    drift = 0.7 * jnp.sin(2.0 * math.pi * 3.0 * position + phases[None, :])
    base_amount = jnp.where(slow_heads, 0.3 / SEQUENCE_TOKENS, 1.0 / 40.0)
    shift_amount = base_amount[None, :] * jnp.exp(spread_part + drift)
    spike_position = jax.random.randint(jax.random.fold_in(key, 105), (2, VALUE_HEADS), 0, SEQUENCE_TOKENS, dtype=jnp.int32)
    token_positions = jnp.arange(SEQUENCE_TOKENS, dtype=jnp.int32)[:, None, None]
    spike_matches = jnp.any(token_positions == spike_position[None, :, :], axis=1)
    spike_magnitude = jax.random.uniform(jax.random.fold_in(key, 106), (SEQUENCE_TOKENS, VALUE_HEADS), jnp.float32, 0.22, 0.69)
    shift_amount = jnp.where(spike_matches, spike_magnitude, shift_amount)
    return jnp.log(jnp.expm1(shift_amount / head_rates[None, :]))


def draw_beta_logit(key, part):
    slow_heads, head_rates = head_plan(key)
    spread_part = jitter(jax.random.fold_in(key, 107))
    slow_beta = 0.4 * DK / SEQUENCE_TOKENS * jnp.exp(spread_part)
    slow_logit = jnp.log(slow_beta) - jnp.log1p(-slow_beta)
    fast_logit = jnp.clip(0.5 + 1.5 * jax.random.normal(jax.random.fold_in(key, 108), (SEQUENCE_TOKENS, VALUE_HEADS), jnp.float32), -5.0, 6.0)
    return jnp.where(slow_heads[None, :], slow_logit, fast_logit)


def block_levels(key, shape, shards, smallest, largest):
    factor_of, own = 1.0, jax.random.fold_in(key, 6)
    for axis_at, shards_of in shards:
        heights = jnp.exp(jax.random.uniform(jax.random.fold_in(own, axis_at), (shards_of,), jnp.float32, smallest / len(shards), largest / len(shards)))
        factor_of = factor_of * jnp.repeat(heights, shape[axis_at] // shards_of).reshape([-1 if axis == axis_at else 1 for axis in range(len(shape))])
    return factor_of


def noise(stream_key, shape, scale, bound, split=(), kind=jnp.bfloat16):
    array = jax.random.normal(stream_key, shape, jnp.float32) * scale
    if len(split) > 0:
        array = block_levels(stream_key, shape, split, -0.22, 0.18) * array
    return jnp.clip(array, min=-bound, max=bound).astype(kind)


def setup_inputs(seed: int = 0) -> dict:
    streams_of = jax.random.split(jax.random.key(seed), 10)
    query = noise(streams_of[0], (SEQUENCE_TOKENS, HK * DK), 1.0, 6.0, ((0, 32), (1, 8)))
    keys = noise(streams_of[1], (SEQUENCE_TOKENS, HK * DK), 1.0, 6.0, ((0, 32), (1, 8)))
    values = noise(streams_of[2], (SEQUENCE_TOKENS, VALUE_HEADS * DV), 1.0, 6.0, ((0, 32), (1, 8)))
    gate_logit = draw_gate_logit(jax.random.fold_in(streams_of[9], 71), 0)
    beta_logit = draw_beta_logit(jax.random.fold_in(streams_of[9], 71), 0)
    decay_rate = draw_decay_rate(jax.random.fold_in(streams_of[9], 71), 0)
    norm_gain = jnp.clip(1.0 + 0.18 * jax.random.normal(streams_of[6], (DV,), jnp.float32), 0.1, 1.9)
    gate_z = noise(streams_of[7], (SEQUENCE_TOKENS, VALUE_HEADS * DV), 1.0, 6.0, ((0, 32), (1, 8)))
    out_weight = noise(streams_of[8], (VALUE_HEADS * DV, D), (VALUE_HEADS * DV) ** -0.5, 0.09375, ((0, 8),))
    return {"query": query, "keys": keys, "values": values, "gate_logit": gate_logit, "beta_logit": beta_logit, "decay_rate": decay_rate, "norm_gain": norm_gain, "gate_z": gate_z, "out_weight": out_weight}


def unit_norm(values_in):
    return values_in * lax.rsqrt(lax.optimization_barrier(jnp.sum(values_in * values_in, axis=-1, keepdims=True)) + 1e-06)

def block_terms(query, keys, values, logdecay, beta):
    highest = lax.Precision.HIGHEST
    size = logdecay.shape[-1]
    width = keys.shape[-1]
    cumul = jnp.cumsum(logdecay, axis=-1)
    differ = cumul[..., :, None] - cumul[..., None, :]
    row_ids = lax.broadcasted_iota(jnp.int32, (size, size), 0)
    col_ids = lax.broadcasted_iota(jnp.int32, (size, size), 1)
    inclusive = col_ids <= row_ids
    strict = col_ids < row_ids
    ratio = jnp.where(inclusive, jnp.exp(jnp.where(inclusive, differ, 0.0)), 0.0)
    key_key = jnp.einsum('...te,...se->...ts', keys, keys, precision=highest)
    query_key = jnp.einsum('...te,...se->...ts', query, keys, precision=highest)
    lower = jnp.where(strict, beta[..., :, None] * ratio * key_key, 0.0) + jnp.eye(size, dtype=jnp.float32)
    rhs_values = beta[..., None] * values
    rhs_keys = (beta * jnp.exp(cumul))[..., None] * keys
    update = lax.linalg.triangular_solve(lower, rhs_values, left_side=True, lower=True, unit_diagonal=True)
    weights = lax.linalg.triangular_solve(lower, rhs_keys, left_side=True, lower=True, unit_diagonal=True)
    mixing = ratio * query_key
    decayed_query = jnp.exp(cumul)[..., None] * query
    key_end = jnp.exp(cumul[..., -1:] - cumul)[..., None] * keys
    transit = jnp.exp(cumul[..., -1])[..., None, None] * jnp.eye(width, dtype=jnp.float32)
    transit = transit - jnp.einsum('...se,...sf->...ef', key_end, weights, precision=highest)
    inject = jnp.einsum('...se,...sf->...ef', key_end, update, precision=highest)
    return (update, weights, mixing, decayed_query, transit, inject)

def run_blocks(terms, start):
    highest = lax.Precision.HIGHEST

    def advance(state, item):
        update, weights, mixing, decayed_query, transit, inject = item
        resid = update - jnp.einsum('...ce,...ef->...cf', weights, state, precision=highest)
        result = jnp.einsum('...ce,...ef->...cf', decayed_query, state, precision=highest)
        result = result + jnp.einsum('...ts,...sf->...tf', mixing, resid, precision=highest)
        state = jnp.einsum('...ef,...fg->...eg', transit, state, precision=highest) + inject
        return (state, result)
    return lax.scan(advance, start, terms)

def reference(query, keys, values, gate_logit, beta_logit, decay_rate, norm_gain, gate_z, out_weight):
    tokens = query.shape[0]
    blocks = tokens // SPAN
    qn = unit_norm(query.astype(jnp.float32).reshape(tokens, HK, DK))
    kn = unit_norm(keys.astype(jnp.float32).reshape(tokens, HK, DK))
    qn = jnp.repeat(qn, 2, axis=1).transpose(1, 0, 2)
    kn = jnp.repeat(kn, 2, axis=1).transpose(1, 0, 2)
    vals = values.astype(jnp.float32).reshape(tokens, VALUE_HEADS, DV).transpose(1, 0, 2)
    logdecay = (-decay_rate[None, :] * jax.nn.softplus(gate_logit)).T
    beta = jax.nn.sigmoid(beta_logit).T

    def one_head(item):
        q_head, k_head, v_head, d_head, b_head = item
        terms = block_terms(q_head.reshape(blocks, SPAN, DK), k_head.reshape(blocks, SPAN, DK), v_head.reshape(blocks, SPAN, DV), d_head.reshape(blocks, SPAN), b_head.reshape(blocks, SPAN))
        final, outs = run_blocks(terms, jnp.zeros((DK, DV), jnp.float32))
        return outs.reshape(tokens, DV)
    core = lax.map(one_head, (qn, kn, vals, logdecay, beta)).transpose(1, 0, 2)
    gate = jax.nn.silu(gate_z.astype(jnp.float32).reshape(tokens, VALUE_HEADS, DV))
    scale = lax.rsqrt(lax.optimization_barrier(jnp.mean(core * core, axis=-1, keepdims=True)) + 1e-06)
    gated = (core * scale * norm_gain * gate).astype(jnp.bfloat16).reshape(tokens, VALUE_HEADS * DV)
    return jnp.dot(gated.astype(jnp.float32), out_weight.astype(jnp.float32), preferred_element_type=jnp.float32).astype(jnp.bfloat16)
```

```python
import jax
import jax.numpy as jnp
from jax import lax
from jax.experimental import pallas as pl
from jax.experimental.pallas import tpu as pltpu
from jax.sharding import PartitionSpec as P

BLK = 128
NB = 4
NH = 4
NY = 4
NZ = 8
NX = 4
ROWS_D = 128
ROWS_C = 144
ROWS_M = 272
F32 = jnp.float32
BF16 = jnp.bfloat16


def dot(left, right):
    return jnp.dot(left, right, preferred_element_type=F32)


def dot_nt(left, right):
    return lax.dot_general(left, right, (((1,), (1,)), ((), ())), preferred_element_type=F32)


def split3(x):
    hi = x.astype(BF16)
    rest = x - hi.astype(F32)
    mid = rest.astype(BF16)
    low = (rest - mid.astype(F32)).astype(BF16)
    return hi, mid, low


def softplus(x):
    y = jnp.exp(-jnp.abs(x))
    small = y * (1.0 - y * (0.5 - y * (1.0 / 3.0 - y * 0.25)))
    return jnp.maximum(x, 0.0) + jnp.where(y < 0.01, small, jnp.log(1.0 + y))


def sigmoid(x):
    return 1.0 / (1.0 + jnp.exp(-x))


def gates(gl_ref, bl_ref, rate_ref, k_ref, q_ref, s):
    g4 = -rate_ref[...] * softplus(gl_ref[...])
    beta4 = sigmoid(bl_ref[...])
    for b in range(NB):
        s["g16"][pl.ds(4 * b, 4), :] = g4[:, BLK * b : BLK * (b + 1)]
    row_ids = lax.broadcasted_iota(jnp.int32, (BLK, BLK), 0)
    col_ids = lax.broadcasted_iota(jnp.int32, (BLK, BLK), 1)
    upper = jnp.where(row_ids <= col_ids, 1.0, 0.0).astype(BF16)
    hi, mid, low = split3(s["g16"][...])
    s["g16"][...] = dot(hi, upper) + dot(mid, upper) + dot(low, upper)
    for b in range(NB):
        for kh in range(2):
            kf = k_ref[pl.ds(BLK * b, BLK), BLK * kh : BLK * (kh + 1)].astype(F32)
            kt = kf.T
            s["kt"][2 * b + kh] = kt.astype(BF16)
            rk = lax.rsqrt(jnp.sum(kt * kt, axis=0, keepdims=True) + 1e-06)
            s["rows"][b, pl.ds(24 + 2 * kh, 1), :] = rk
            s["rows"][b, pl.ds(25 + 2 * kh, 1), :] = rk
            qf = q_ref[pl.ds(BLK * b, BLK), BLK * kh : BLK * (kh + 1)].astype(F32)
            s["rq"][kh, pl.ds(BLK * b, BLK), :] = lax.rsqrt(
                jnp.sum(qf * qf, axis=1, keepdims=True) + 1e-06
            )
        c = s["g16"][pl.ds(4 * b, 4), :]
        beta = beta4[:, BLK * b : BLK * (b + 1)]
        rk4 = s["rows"][b, pl.ds(24, 4), :]
        end = c[:, BLK - 1 : BLK]
        ec = jnp.exp(c)
        s["rows"][b, pl.ds(0, 4), :] = c
        s["rows"][b, pl.ds(4, 4), :] = beta * rk4
        s["rows"][b, pl.ds(8, 4), :] = rk4 * jnp.exp(end - c)
        s["rows"][b, pl.ds(12, 4), :] = ec
        s["rows"][b, pl.ds(16, 4), :] = beta
        s["rows"][b, pl.ds(20, 4), :] = beta * rk4 * ec
        s["rows"][b, pl.ds(28, 4), :] = jnp.exp(jnp.broadcast_to(end, (4, BLK)))
        s["cols"][b] = s["rows"][b].T


def block_terms(k_ref, q_ref, v_ref, s):
    row_ids = lax.broadcasted_iota(jnp.int32, (BLK, BLK), 0)
    col_ids = lax.broadcasted_iota(jnp.int32, (BLK, BLK), 1)
    inclusive = col_ids <= row_ids
    differ = row_ids ^ col_ids
    ident = jnp.where(row_ids == col_ids, 1.0, 0.0)

    def group(g, carry):
        lower = {}
        for i in range(2):
            b = 2 * g + i
            tok = pl.ds(pl.multiple_of(b * BLK, BLK), BLK)
            cols = s["cols"][b]
            for kh in range(2):
                kt = s["kt"][2 * b + kh]
                kk = dot(k_ref[tok, BLK * kh : BLK * (kh + 1)], kt)
                qk = dot(q_ref[tok, BLK * kh : BLK * (kh + 1)], kt)
                rk = s["rows"][b, pl.ds(24 + 2 * kh, 1), :]
                for h in (2 * kh, 2 * kh + 1):
                    gap = cols[:, h : h + 1] - s["rows"][b, pl.ds(h, 1), :]
                    ratio = jnp.exp(jnp.where(inclusive, gap, -1e30)) * rk
                    s["mix"][4 * b + h] = (ratio * qk).astype(BF16)
                    lower[i, h] = cols[:, 4 + h : 5 + h] * ratio * kk
                    s["low"][4 * i + h] = lower[i, h]
        pairs = [(i, h) for i in range(2) for h in range(NH)]
        for p in pairs:
            off = jnp.where(differ == 1, s["low"][4 * p[0] + p[1]], 0.0)
            s["inv"][4 * p[0] + p[1]] = ident - off
        for level in range(1, 7):
            here = (differ >> level) == 1
            part = {}
            for p in pairs:
                n = 4 * p[0] + p[1]
                off = jnp.where(here, s["low"][n], 0.0).astype(BF16)
                part[p] = dot(off, s["inv"][n].astype(BF16)).astype(BF16)
            for p in pairs:
                n = 4 * p[0] + p[1]
                inv = s["inv"][n]
                s["inv"][n] = inv - dot(inv.astype(BF16), part[p])
        for i, h in pairs:
            b = 2 * g + i
            tok = pl.ds(pl.multiple_of(b * BLK, BLK), BLK)
            inv = s["inv"][4 * i + h]
            t_v = (inv * s["rows"][b, pl.ds(16 + h, 1), :]).astype(BF16)
            t_k = (inv * s["rows"][b, pl.ds(20 + h, 1), :]).astype(BF16)
            kh = h // 2
            s["upd"][4 * b + h] = dot(t_v, v_ref[tok, BLK * h : BLK * (h + 1)])
            s["wts"][4 * b + h] = dot(t_k, k_ref[tok, BLK * kh : BLK * (kh + 1)]).astype(BF16)
        return carry

    lax.fori_loop(0, NB // 2, group, 0)


def run_shard(s):
    row_ids = lax.broadcasted_iota(jnp.int32, (BLK, BLK), 0)
    col_ids = lax.broadcasted_iota(jnp.int32, (BLK, BLK), 1)
    eye = row_ids == col_ids
    for h in range(NH):
        s["state"][h, :, :BLK] = jnp.zeros((BLK, BLK), F32)
        s["state"][h, :, BLK:] = jnp.where(eye, 1.0, 0.0)

    def block(b, carry):
        cols = s["cols"][b]
        for h in range(NH):
            n = 4 * b + h
            state = s["state"][h].astype(BF16)
            s["sb"][n] = state
            ws = dot(s["wts"][n], state)
            res_s = s["upd"][n] - ws[:, :BLK]
            res_a = -ws[:, BLK:]
            end = cols[:, 8 + h : 9 + h]
            s["rb"][n, :, :BLK] = res_s.astype(BF16)
            s["rb"][n, :, BLK:] = res_a.astype(BF16)
            s["re"][h, :, :BLK] = (end * res_s).astype(BF16)
            s["re"][h, :, BLK:] = (end * res_a).astype(BF16)
        for h in range(NH):
            gain = s["rows"][b, pl.ds(28 + h, 1), :]
            grow = dot(s["kt"][2 * b + h // 2], s["re"][h])
            s["state"][h, :, :BLK] = gain * s["state"][h, :, :BLK] + grow[:, :BLK]
            s["state"][h, :, BLK:] = gain * s["state"][h, :, BLK:] + grow[:, BLK:]
        return carry

    lax.fori_loop(0, NB, block, 0)
    c_ids = lax.broadcasted_iota(jnp.int32, (16, BLK), 0)
    for h in range(NH):
        total = s["g16"][pl.ds(h, 1), :]
        for b in range(1, NB):
            total = total + s["g16"][pl.ds(4 * b + h, 1), :]
        c = jnp.exp(jnp.broadcast_to(total[:, BLK - 1 : BLK], (16, BLK)))
        hi, mid, low = (part.astype(F32) for part in split3(c))
        terms = jnp.where(c_ids == 0, hi, jnp.where(c_ids == 1, mid, jnp.where(c_ids == 2, low, 0.0)))
        fix = jnp.where(eye, c[:1], 0.0) - s["state"][h, :, BLK:]
        s["msg"][h, :ROWS_D, :] = fix.T.astype(BF16)
        s["msg"][h, ROWS_D:ROWS_C, :] = terms.astype(BF16)
        s["msg"][h, ROWS_C:, :] = s["state"][h, :, :BLK].T.astype(BF16)


def block_output(b, q_ref, s):
    tok = pl.ds(b * BLK, BLK)
    for h in range(NH):
        n = 4 * b + h
        kh = h // 2
        qs = dot(q_ref[tok, BLK * kh : BLK * (kh + 1)], s["sb"][n])
        out = s["cols"][b, :, 12 + h : 13 + h] * qs + dot(s["mix"][n], s["rb"][n])
        s["oloc"][h, tok, :] = out[:, :BLK]
        s["corr"][h, tok, :] = out[:, BLK:].astype(BF16)


def kernel(
    q_ref, k_ref, v_ref, gl_ref, bl_ref, rate_ref, gain_ref, z_hbm, w_hbm, out_ref,
    g16, rows, cols, rq, kt, mix, low, inv, upd, wts, state, sb, rb, re, msg, oloc, corr,
    z_buf, w_buf, gate, dball, bst, xst, xr, xin, gated, parta, recva, partb, sumb, recvb,
    load_sem, y_send, y_recv, rr_send, rr_recv, rl_send, rl_recv, b_send, b_recv,
    u_send, u_recv, x_send, x_recv, a_send, a_recv, e_send, e_recv,
):
    s = dict(
        g16=g16, rows=rows, cols=cols, rq=rq, kt=kt, mix=mix, low=low, inv=inv, upd=upd, wts=wts,
        state=state, sb=sb, rb=rb, re=re, msg=msg, oloc=oloc, corr=corr,
    )
    seq = lax.axis_index("seq")
    head = lax.axis_index("head")
    y, z = seq // NZ, seq % NZ
    x, core = head // 2, head % 2

    def at(y_to, z_to):
        return (y_to * NZ + z_to, head)

    def on_line(x_to, core_to):
        return (seq, 2 * x_to + core_to)

    def remote(src, dst, send, recv, device):
        return pltpu.make_async_remote_copy(
            src_ref=src, dst_ref=dst, send_sem=send, recv_sem=recv,
            device_id=device, device_id_type=pl.DeviceIdType.MESH,
        )

    peers = [at((y + i) % NY, z) for i in range(1, NY)]
    peers += [at(y, (z + i) % NZ) for i in range(1, NZ)]
    peers += [on_line((x + i) % NX, core) for i in range(1, NX)]
    peers += [on_line(x, 1 - core)]
    barrier = pltpu.get_barrier_semaphore()
    for peer in peers:
        pl.semaphore_signal(barrier, inc=1, device_id=peer, device_id_type=pl.DeviceIdType.MESH)
    load_z = pltpu.make_async_copy(z_hbm, z_buf, load_sem.at[0])
    load_w = pltpu.make_async_copy(w_hbm, w_buf, load_sem.at[1])
    load_z.start()
    load_w.start()

    with jax.named_scope("local_terms"):
        gates(gl_ref, bl_ref, rate_ref, k_ref, q_ref, s)
        block_terms(k_ref, q_ref, v_ref, s)
        run_shard(s)

    pl.semaphore_wait(barrier, len(peers))
    sends = []

    def go(copy):
        copy.start()
        sends.append(copy)

    for i in range(1, NY):
        to = (y + i) % NY
        go(remote(msg.at[to], dball.at[y, z], y_send.at[i - 1], y_recv.at[i - 1], at(to, z)))
    dball[y, z] = msg[y]
    block_output(0, q_ref, s)
    for i in range(1, NY):
        remote(msg.at[0], dball.at[(y + NY - i) % NY, z], y_send.at[i - 1], y_recv.at[i - 1], at(y, z)).wait_recv()

    for i in range(1, NZ):
        to = (z + i) % NZ
        piece = pl.ds(pl.multiple_of(ROWS_C + 16 * to, 16), 16)
        go(remote(dball.at[:, z, piece, :], bst.at[:, z], b_send.at[i - 1], b_recv.at[i - 1], at(y, to)))
    own = pl.ds(pl.multiple_of(ROWS_C + 16 * z, 16), 16)
    for r in range(NY):
        bst[r, z] = dball[r, z, own, :]

    right, left = (z + 1) % NZ, (z + NZ - 1) % NZ

    def ring(level):
        for r in range(NY):
            if level < 4 or r % 2 == 0:
                slot = dball.at[r, (z + NZ - level + 1) % NZ, :ROWS_C, :]
                go(remote(slot, slot, rr_send.at[level - 1, r], rr_recv.at[level - 1, r], at(y, right)))
            if level < 4 or r % 2 == 1:
                slot = dball.at[r, (z + level - 1) % NZ, :ROWS_C, :]
                go(remote(slot, slot, rl_send.at[level - 1, r], rl_recv.at[level - 1, r], at(y, left)))

    def ring_wait(level):
        for r in range(NY):
            if level < 4 or r % 2 == 0:
                slot = dball.at[r, (z + NZ - level) % NZ, :ROWS_C, :]
                remote(slot, slot, rr_send.at[level - 1, r], rr_recv.at[level - 1, r], at(y, right)).wait_recv()
            if level < 4 or r % 2 == 1:
                slot = dball.at[r, (z + level) % NZ, :ROWS_C, :]
                remote(slot, slot, rl_send.at[level - 1, r], rl_recv.at[level - 1, r], at(y, left)).wait_recv()

    ring(1)
    for level in range(1, 4):
        block_output(level, q_ref, s)
        ring_wait(level)
        ring(level + 1)
    load_z.wait()
    zf = z_buf[...].astype(F32)
    zs = zf * sigmoid(zf)
    for h in range(NH):
        gate[:, BLK * h : BLK * (h + 1)] = zs[:, BLK * h : BLK * (h + 1)] * gain_ref[...]
    ring_wait(4)
    for i in range(1, NZ):
        remote(
            dball.at[:, z, :16, :], bst.at[:, (z + NZ - i) % NZ], b_send.at[i - 1], b_recv.at[i - 1], at(y, z)
        ).wait_recv()

    carry = jnp.zeros((16, BLK), F32)
    for r in range(NY):
        for j in range(NZ):
            xst[r, j] = carry.astype(BF16)
            if r == NY - 1 and j == NZ - 1:
                break
            c = jnp.sum(dball[r, j, ROWS_D:ROWS_C, :].astype(F32), axis=0, keepdims=True)
            carry = c * carry - dot(carry.astype(BF16), dball[r, j, :ROWS_D, :]) + bst[r, j].astype(F32)

        @pl.when(y != r)
        def _():
            remote(xst.at[r], xr.at[y], u_send.at[r], u_recv.at[y], at(r, z)).start()

        @pl.when(y == r)
        def _():
            xr[y] = xst[r]

    for i in range(1, NY):
        source = (y + i) % NY
        remote(xst.at[0], xr.at[source], u_send.at[0], u_recv.at[source], at(y, z)).wait_recv()
    for i in range(1, NZ):
        to = (z + i) % NZ
        go(remote(xr.at[:, to], xin.at[:, z], x_send.at[i - 1], x_recv.at[i - 1], at(y, to)))
    for h in range(NH):
        xin[h, z] = xr[h, z]
    for i in range(1, NZ):
        remote(
            xr.at[:, z], xin.at[:, (z + NZ - i) % NZ], x_send.at[i - 1], x_recv.at[i - 1], at(y, z)
        ).wait_recv()

    load_w.wait()

    def gate_half(which):
        for h in range(NH):
            start = xin[h].reshape(BLK, BLK)
            for j in range(NX):
                tok = pl.ds(pl.multiple_of((2 * j + which) * 64, 64), 64)
                core_out = oloc[h, tok, :] + dot_nt(corr[h, tok, :], start)
                r = rq[h // 2, tok, :]
                mean = jnp.mean(core_out * core_out, axis=1, keepdims=True)
                scale = r * lax.rsqrt(r * r * mean + 1e-06)
                lanes = slice(BLK * h, BLK * (h + 1))
                gated[64 * j : 64 * (j + 1), lanes] = (core_out * scale * gate[tok, lanes]).astype(BF16)

    gate_half(1 - core)
    for n in range(4):
        parta[n] = dot(gated[...], w_buf[:, 512 * n : 512 * (n + 1)]).astype(BF16)
        go(remote(parta.at[n], recva.at[n], a_send.at[n], a_recv.at[n], on_line(x, 1 - core)))
    gate_half(core)
    for n in range(4):
        partb[n] = dot(gated[...], w_buf[:, 512 * n : 512 * (n + 1)])
        remote(parta.at[n], recva.at[n], a_send.at[n], a_recv.at[n], on_line(x, core)).wait_recv()
        partb[n] = partb[n] + recva[n].astype(F32)
        sumb[n] = partb[n].astype(BF16)
        for i in range(1, NX):
            to = (x + i) % NX
            rows_to = pl.ds(pl.multiple_of(64 * to, 64), 64)
            go(remote(sumb.at[n, rows_to, :], recvb.at[n, i - 1], e_send.at[n, i - 1], e_recv.at[n, i - 1], on_line(to, core)))
    mine = pl.ds(pl.multiple_of(64 * x, 64), 64)
    for n in range(4):
        total = partb[n, mine, :]
        for i in range(1, NX):
            remote(
                sumb.at[n, mine, :], recvb.at[n, i - 1], e_send.at[n, i - 1], e_recv.at[n, i - 1], on_line(x, core)
            ).wait_recv()
            total = total + recvb[n, i - 1].astype(F32)
        out_ref[:, 512 * n : 512 * (n + 1)] = total.astype(BF16)

    for copy in sends:
        copy.wait_send()
    for r in range(NY):

        @pl.when(y != r)
        def _():
            remote(xst.at[r], xr.at[y], u_send.at[r], u_recv.at[y], at(r, z)).wait_send()


def on_device(query, keys, values, gate_logit, beta_logit, decay_rate, norm_gain, gate_z, out_weight):
    vmem = pl.BlockSpec(memory_space=pltpu.VMEM)
    anywhere = pl.BlockSpec(memory_space=pl.ANY)
    dma = pltpu.SemaphoreType.DMA
    pairs = NB * NH
    scratch = [
        pltpu.VMEM((16, BLK), F32),
        pltpu.VMEM((NB, 32, BLK), F32),
        pltpu.VMEM((NB, BLK, 32), F32),
        pltpu.VMEM((2, 512, 1), F32),
        pltpu.VMEM((2 * NB, BLK, BLK), BF16),
        pltpu.VMEM((pairs, BLK, BLK), BF16),
        pltpu.VMEM((8, BLK, BLK), F32),
        pltpu.VMEM((8, BLK, BLK), F32),
        pltpu.VMEM((pairs, BLK, BLK), F32),
        pltpu.VMEM((pairs, BLK, BLK), BF16),
        pltpu.VMEM((NH, BLK, 2 * BLK), F32),
        pltpu.VMEM((pairs, BLK, 2 * BLK), BF16),
        pltpu.VMEM((pairs, BLK, 2 * BLK), BF16),
        pltpu.VMEM((NH, BLK, 2 * BLK), BF16),
        pltpu.VMEM((NH, ROWS_M, BLK), BF16),
        pltpu.VMEM((NH, 512, BLK), F32),
        pltpu.VMEM((NH, 512, BLK), BF16),
        pltpu.VMEM((512, 512), BF16),
        pltpu.VMEM((512, 2048), BF16),
        pltpu.VMEM((512, 512), F32),
        pltpu.VMEM((NY, NZ, ROWS_M, BLK), BF16),
        pltpu.VMEM((NY, NZ, 16, BLK), BF16),
        pltpu.VMEM((NY, NZ, 16, BLK), BF16),
        pltpu.VMEM((NH, NZ, 16, BLK), BF16),
        pltpu.VMEM((NH, NZ, 16, BLK), BF16),
        pltpu.VMEM((256, 512), BF16),
        pltpu.VMEM((4, 256, 512), BF16),
        pltpu.VMEM((4, 256, 512), BF16),
        pltpu.VMEM((4, 256, 512), F32),
        pltpu.VMEM((4, 256, 512), BF16),
        pltpu.VMEM((4, 3, 64, 512), BF16),
        dma((2,)),
        dma((3,)), dma((3,)),
        dma((4, 4)), dma((4, 4)), dma((4, 4)), dma((4, 4)),
        dma((7,)), dma((7,)),
        dma((4,)), dma((4,)),
        dma((7,)), dma((7,)),
        dma((4,)), dma((4,)),
        dma((4, 3)), dma((4, 3)),
    ]
    return pl.pallas_call(
        kernel,
        out_shape=jax.ShapeDtypeStruct((64, 2048), BF16),
        in_specs=[vmem] * 7 + [anywhere] * 2,
        out_specs=vmem,
        scratch_shapes=scratch,
        compiler_params=pltpu.CompilerParams(
            collective_id=0, has_side_effects=True, vmem_limit_bytes=48 * 1024 * 1024
        ),
    )(
        query, keys, values, gate_logit.T, beta_logit.T, decay_rate.reshape(NH, 1),
        norm_gain.reshape(1, BLK), gate_z, out_weight,
    )


def solution(mesh):
    return jax.shard_map(
        on_device,
        mesh=mesh,
        in_specs=(
            P("seq", "head"),
            P("seq", "head"),
            P("seq", "head"),
            P("seq", "head"),
            P("seq", "head"),
            P("head"),
            P(),
            P("seq", "head"),
            P("head", None),
        ),
        out_specs=P(("seq", "head"), None),
        check_vma=False,
    )
```

```python
import jax
import jax.numpy as jnp
from jax import lax
from jax.experimental import pallas as pl
from jax.experimental.pallas import tpu as pltpu
from jax.sharding import PartitionSpec as P

BLK = 128
NB = 4
NH = 4
NY = 4
NZ = 8
NX = 4
ROWS_D = 128
ROWS_C = 144
ROWS_M = 272
TREE = (
    (0, 0, None), (4, 0, 12), (2, 0, 8), (1, 0, 0), (6, 4, 10), (5, 4, 4), (3, 2, 2), (7, 6, 6),
)
F32 = jnp.float32
BF16 = jnp.bfloat16


def dot(left, right):
    return jnp.dot(left, right, preferred_element_type=F32)


def dot_nt(left, right):
    return lax.dot_general(left, right, (((1,), (1,)), ((), ())), preferred_element_type=F32)


def split3(x):
    hi = x.astype(BF16)
    rest = x - hi.astype(F32)
    mid = rest.astype(BF16)
    low = (rest - mid.astype(F32)).astype(BF16)
    return hi, mid, low


def softplus(x):
    y = jnp.exp(-jnp.abs(x))
    small = y * (1.0 - y * (0.5 - y * (1.0 / 3.0 - y * 0.25)))
    return jnp.maximum(x, 0.0) + jnp.where(y < 0.01, small, jnp.log(1.0 + y))


def sigmoid(x):
    return 1.0 / (1.0 + jnp.exp(-x))


def gates(gl_ref, bl_ref, rate_ref, k_ref, q_ref, s):
    same = lax.broadcasted_iota(jnp.int32, (NH, NH), 0) == lax.broadcasted_iota(jnp.int32, (NH, NH), 1)
    rate = jnp.sum(jnp.where(same, rate_ref[...], 0.0), axis=1, keepdims=True)
    g4 = -rate * softplus(gl_ref[...])
    beta4 = sigmoid(bl_ref[...])
    for b in range(NB):
        s["g16"][pl.ds(4 * b, 4), :] = g4[:, BLK * b : BLK * (b + 1)]
    row_ids = lax.broadcasted_iota(jnp.int32, (BLK, BLK), 0)
    col_ids = lax.broadcasted_iota(jnp.int32, (BLK, BLK), 1)
    upper = jnp.where(row_ids <= col_ids, 1.0, 0.0).astype(BF16)
    hi, mid, low = split3(s["g16"][...])
    s["g16"][...] = dot(hi, upper) + dot(mid, upper) + dot(low, upper)
    for b in range(NB):
        for kh in range(2):
            kf = k_ref[pl.ds(BLK * b, BLK), BLK * kh : BLK * (kh + 1)].astype(F32)
            kt = kf.T
            s["kt"][2 * b + kh] = kt.astype(BF16)
            rk = lax.rsqrt(jnp.sum(kt * kt, axis=0, keepdims=True) + 1e-06)
            s["rows"][b, pl.ds(24 + 2 * kh, 1), :] = rk
            s["rows"][b, pl.ds(25 + 2 * kh, 1), :] = rk
            qf = q_ref[pl.ds(BLK * b, BLK), BLK * kh : BLK * (kh + 1)].astype(F32)
            s["rq"][kh, pl.ds(BLK * b, BLK), :] = lax.rsqrt(
                jnp.sum(qf * qf, axis=1, keepdims=True) + 1e-06
            )
        c = s["g16"][pl.ds(4 * b, 4), :]
        beta = beta4[:, BLK * b : BLK * (b + 1)]
        rk4 = s["rows"][b, pl.ds(24, 4), :]
        end = c[:, BLK - 1 : BLK]
        ec = jnp.exp(c)
        s["rows"][b, pl.ds(0, 4), :] = c
        s["rows"][b, pl.ds(4, 4), :] = beta * rk4
        s["rows"][b, pl.ds(8, 4), :] = rk4 * jnp.exp(end - c)
        s["rows"][b, pl.ds(12, 4), :] = ec
        s["rows"][b, pl.ds(16, 4), :] = beta
        s["rows"][b, pl.ds(20, 4), :] = beta * rk4 * ec
        s["rows"][b, pl.ds(28, 4), :] = jnp.exp(jnp.broadcast_to(end, (4, BLK)))
        s["cols"][b] = s["rows"][b].T


def block_terms(k_ref, q_ref, v_ref, s):
    row_ids = lax.broadcasted_iota(jnp.int32, (BLK, BLK), 0)
    col_ids = lax.broadcasted_iota(jnp.int32, (BLK, BLK), 1)
    inclusive = col_ids <= row_ids
    differ = row_ids ^ col_ids
    ident = jnp.where(row_ids == col_ids, 1.0, 0.0)

    def group(g, carry):
        lower = {}
        for i in range(2):
            b = 2 * g + i
            tok = pl.ds(pl.multiple_of(b * BLK, BLK), BLK)
            cols = s["cols"][b]
            for kh in range(2):
                kt = s["kt"][2 * b + kh]
                kk = dot(k_ref[tok, BLK * kh : BLK * (kh + 1)], kt)
                qk = dot(q_ref[tok, BLK * kh : BLK * (kh + 1)], kt)
                rk = s["rows"][b, pl.ds(24 + 2 * kh, 1), :]
                for h in (2 * kh, 2 * kh + 1):
                    gap = cols[:, h : h + 1] - s["rows"][b, pl.ds(h, 1), :]
                    ratio = jnp.exp(jnp.where(inclusive, gap, -1e30)) * rk
                    s["mix"][4 * b + h] = (ratio * qk).astype(BF16)
                    lower[i, h] = cols[:, 4 + h : 5 + h] * ratio * kk
                    s["low"][4 * i + h] = lower[i, h]
        pairs = [(i, h) for i in range(2) for h in range(NH)]
        for p in pairs:
            off = jnp.where(differ == 1, s["low"][4 * p[0] + p[1]], 0.0)
            s["inv"][4 * p[0] + p[1]] = ident - off
        for level in range(1, 7):
            here = (differ >> level) == 1
            part = {}
            for p in pairs:
                n = 4 * p[0] + p[1]
                off = jnp.where(here, s["low"][n], 0.0).astype(BF16)
                part[p] = dot(off, s["inv"][n].astype(BF16)).astype(BF16)
            for p in pairs:
                n = 4 * p[0] + p[1]
                inv = s["inv"][n]
                s["inv"][n] = inv - dot(inv.astype(BF16), part[p])
        for i, h in pairs:
            b = 2 * g + i
            tok = pl.ds(pl.multiple_of(b * BLK, BLK), BLK)
            inv = s["inv"][4 * i + h]
            t_v = (inv * s["rows"][b, pl.ds(16 + h, 1), :]).astype(BF16)
            t_k = (inv * s["rows"][b, pl.ds(20 + h, 1), :]).astype(BF16)
            kh = h // 2
            s["upd"][4 * b + h] = dot(t_v, v_ref[tok, BLK * h : BLK * (h + 1)])
            s["wts"][4 * b + h] = dot(t_k, k_ref[tok, BLK * kh : BLK * (kh + 1)]).astype(BF16)
        return carry

    lax.fori_loop(0, NB // 2, group, 0)


def run_shard(s):
    row_ids = lax.broadcasted_iota(jnp.int32, (BLK, BLK), 0)
    col_ids = lax.broadcasted_iota(jnp.int32, (BLK, BLK), 1)
    eye = row_ids == col_ids
    for h in range(NH):
        s["state"][h, :, :BLK] = jnp.zeros((BLK, BLK), F32)
        s["state"][h, :, BLK:] = jnp.where(eye, 1.0, 0.0)

    def block(b, carry):
        cols = s["cols"][b]
        for h in range(NH):
            n = 4 * b + h
            state = s["state"][h].astype(BF16)
            s["sb"][n] = state
            ws = dot(s["wts"][n], state)
            res_s = s["upd"][n] - ws[:, :BLK]
            res_a = -ws[:, BLK:]
            end = cols[:, 8 + h : 9 + h]
            s["rb"][n, :, :BLK] = res_s.astype(BF16)
            s["rb"][n, :, BLK:] = res_a.astype(BF16)
            s["re"][h, :, :BLK] = (end * res_s).astype(BF16)
            s["re"][h, :, BLK:] = (end * res_a).astype(BF16)
        for h in range(NH):
            gain = s["rows"][b, pl.ds(28 + h, 1), :]
            grow = dot(s["kt"][2 * b + h // 2], s["re"][h])
            s["state"][h, :, :BLK] = gain * s["state"][h, :, :BLK] + grow[:, :BLK]
            s["state"][h, :, BLK:] = gain * s["state"][h, :, BLK:] + grow[:, BLK:]
        return carry

    lax.fori_loop(0, NB, block, 0)


def write_message(ref, c, fix, inject):
    c_ids = lax.broadcasted_iota(jnp.int32, (16, BLK), 0)
    hi, mid, low = (part.astype(F32) for part in split3(jnp.broadcast_to(c, (16, BLK))))
    terms = jnp.where(c_ids == 0, hi, jnp.where(c_ids == 1, mid, jnp.where(c_ids == 2, low, 0.0)))
    ref[:ROWS_D, :] = fix.astype(BF16)
    ref[ROWS_D:ROWS_C, :] = terms.astype(BF16)
    ref[ROWS_C:, :] = inject.astype(BF16)


def decay_of(ref):
    return jnp.sum(ref[ROWS_D:ROWS_C, :].astype(F32), axis=0, keepdims=True)


def compose(first, second, out):
    c_1, c_2 = decay_of(first), decay_of(second)
    prod = dot(first[...], second[:ROWS_D, :])
    fix = c_2 * first[:ROWS_D, :].astype(F32) + c_1 * second[:ROWS_D, :].astype(F32) - prod[:ROWS_D]
    inject = c_2 * first[ROWS_C:, :].astype(F32) + second[ROWS_C:, :].astype(F32) - prod[ROWS_C:]
    write_message(out, c_1 * c_2, fix, inject)


def step(ref, state):
    moved = decay_of(ref) * state - dot(state.astype(BF16), ref[:ROWS_D, :])
    return moved + ref[ROWS_C:, :].astype(F32)


def block_output(b, q_ref, s):
    tok = pl.ds(b * BLK, BLK)
    for h in range(NH):
        n = 4 * b + h
        kh = h // 2
        qs = dot(q_ref[tok, BLK * kh : BLK * (kh + 1)], s["sb"][n])
        out = s["cols"][b, :, 12 + h : 13 + h] * qs + dot(s["mix"][n], s["rb"][n])
        s["oloc"][h, tok, :] = out[:, :BLK]
        s["corr"][h, tok, :] = out[:, BLK:].astype(BF16)


def kernel(
    q_hbm, k_hbm, v_hbm, gl_hbm, bl_hbm, rate_hbm, gain_hbm, z_hbm, w_hbm, out_ref,
    q_ref, k_ref, v_ref, gl_ref, bl_ref, rate_ref, gain_ref, z_buf, w_buf,
    g16, rows, cols, rq, kt, mix, low, inv, upd, wts, state, sb, rb, re, msg, oloc, corr,
    gate, parts, rmsg, rowbuf, start, xst, xin,
    gated, parta, recva, partb, sumb, relay, hop, recvb,
    load_sem, m_send, m_recv, r_send, r_recv, x_send, x_recv,
    a_send, a_recv, f_send, f_recv, e_send, e_recv,
):
    s = dict(
        g16=g16, rows=rows, cols=cols, rq=rq, kt=kt, mix=mix, low=low, inv=inv, upd=upd, wts=wts,
        state=state, sb=sb, rb=rb, re=re, msg=msg, oloc=oloc, corr=corr,
    )
    loads = [
        pltpu.make_async_copy(src, dst, load_sem.at[i])
        for i, (src, dst) in enumerate([
            (gl_hbm, gl_ref), (bl_hbm, bl_ref), (rate_hbm, rate_ref), (k_hbm, k_ref), (q_hbm, q_ref),
            (v_hbm, v_ref), (gain_hbm, gain_ref), (z_hbm, z_buf), (w_hbm, w_buf),
        ])
    ]
    for load in loads:
        load.start()
    seq = lax.axis_index("seq")
    head = lax.axis_index("head")
    y, z = seq // NZ, seq % NZ
    x, core = head // 2, head % 2
    mine = z // 2
    owns = z % 2 == core

    def at(y_to, z_to):
        return (y_to * NZ + z_to, head)

    def owner(h):
        return at(y, 2 * h + core)

    def on_line(x_to, core_to):
        return (seq, 2 * x_to + core_to)

    def remote(src, dst, send, recv, device):
        return pltpu.make_async_remote_copy(
            src_ref=src, dst_ref=dst, send_sem=send, recv_sem=recv,
            device_id=device, device_id_type=pl.DeviceIdType.MESH,
        )

    ahead, behind = (x + 1) % NX, (x + NX - 1) % NX
    peers = [at(y, (z + i) % NZ) for i in range(1, NZ)]
    peers += [at((y + i) % NY, z) for i in range(1, NY)]
    peers += [on_line(ahead, core), on_line(behind, core), on_line(x, 1 - core)]
    barrier = pltpu.get_barrier_semaphore()
    for peer in peers:
        pl.semaphore_signal(barrier, inc=1, device_id=peer, device_id_type=pl.DeviceIdType.MESH)
    for load in loads[:6]:
        load.wait()

    gates(gl_ref, bl_ref, rate_ref, k_ref, q_ref, s)
    block_terms(k_ref, q_ref, v_ref, s)
    run_shard(s)
    pl.semaphore_wait(barrier, len(peers))
    sends = []

    def go(copy):
        copy.start()
        sends.append(copy)

    row_ids = lax.broadcasted_iota(jnp.int32, (BLK, BLK), 0)
    eye = row_ids == lax.broadcasted_iota(jnp.int32, (BLK, BLK), 1)
    for h in range(NH):
        total = g16[pl.ds(h, 1), :]
        for b in range(1, NB):
            total = total + g16[pl.ds(4 * b + h, 1), :]
        c = jnp.exp(jnp.broadcast_to(total[:, BLK - 1 : BLK], (1, BLK)))
        fix = jnp.where(eye, c, 0.0) - state[h, :, BLK:]
        write_message(msg.at[h], c, fix.T, state[h, :, :BLK].T)

        @pl.when(z != 2 * h + core)
        def _():
            remote(msg.at[h], parts.at[z], m_send.at[h], m_recv.at[z], owner(h)).start()

        @pl.when(z == 2 * h + core)
        def _():
            parts[z] = msg[h]

    for b in range(NB):
        block_output(b, q_ref, s)
    for load in loads[6:]:
        load.wait()
    zf = z_buf[...].astype(F32)
    zs = zf * sigmoid(zf)
    for h in range(NH):
        gate[:, BLK * h : BLK * (h + 1)] = zs[:, BLK * h : BLK * (h + 1)] * gain_ref[...]

    @pl.when(owns)
    def _():
        for k in range(4):
            for j in (2 * k, 2 * k + 1):

                @pl.when(z != j)
                def _():
                    remote(msg.at[0], parts.at[j], m_send.at[0], m_recv.at[j], at(y, z)).wait_recv()

            compose(parts.at[2 * k], parts.at[2 * k + 1], parts.at[8 + k])
        for k in range(2):
            compose(parts.at[8 + 2 * k], parts.at[9 + 2 * k], parts.at[12 + k])
        compose(parts.at[12], parts.at[13], rmsg)
        for i in range(NY - 1, 0, -1):

            @pl.when(y + i < NY)
            def _():
                remote(rmsg, rowbuf.at[y], r_send.at[i - 1], r_recv.at[y], at((y + i) % NY, z)).start()

        start[...] = jnp.zeros_like(start)
        for r in range(NY - 1):

            @pl.when(r < y)
            def _():
                remote(rmsg, rowbuf.at[r], r_send.at[0], r_recv.at[r], at(y, z)).wait_recv()
                if r == 0:
                    start[...] = rowbuf[r, ROWS_C:, :].astype(F32)
                else:
                    start[...] = step(rowbuf.at[r], start[...])

        states = {0: start[...]}
        for j, source, stretch in TREE:
            if stretch is not None:
                states[j] = step(parts.at[stretch], states[source])
            xst[j] = states[j].astype(BF16)

            @pl.when(j != z)
            def _():
                remote(xst.at[j], xin.at[mine], x_send.at[j], x_recv.at[mine], at(y, j)).start()

            @pl.when(j == z)
            def _():
                xin[mine] = xst[j]

    for h in range(NH):

        @pl.when(z != 2 * h + core)
        def _():
            remote(xst.at[0], xin.at[h], x_send.at[0], x_recv.at[h], at(y, z)).wait_recv()

    def gate_half(which):
        for h in range(NH):
            for j in range(NX):
                tok = pl.ds(pl.multiple_of((2 * j + which) * 64, 64), 64)
                core_out = oloc[h, tok, :] + dot_nt(corr[h, tok, :], xin[h])
                r = rq[h // 2, tok, :]
                mean = jnp.mean(core_out * core_out, axis=1, keepdims=True)
                scale = r * lax.rsqrt(r * r * mean + 1e-06)
                lanes = slice(BLK * h, BLK * (h + 1))
                gated[64 * j : 64 * (j + 1), lanes] = (core_out * scale * gate[tok, lanes]).astype(BF16)

    order = (0, 2, 1, 3)
    gate_half(1 - core)
    for n in order:
        parta[n] = dot(gated[...], w_buf[:, 512 * n : 512 * (n + 1)]).astype(BF16)
        go(remote(parta.at[n], recva.at[n], a_send.at[n], a_recv.at[n], on_line(x, 1 - core)))
    gate_half(core)

    def rows_of(chip):
        return pl.ds(pl.multiple_of(64 * chip, 64), 64)

    def ways(n):
        return (ahead, behind) if n < 2 else (behind, ahead)

    def send_on(n):
        onward, back = ways(n)
        remote(sumb.at[n, rows_of(x), :], relay.at[n], f_send.at[n], f_recv.at[n], on_line(x, core)).wait_recv()
        hop[n] = (partb[n, rows_of(onward), :] + relay[n].astype(F32)).astype(BF16)
        go(remote(hop.at[n], recvb.at[n, 1], e_send.at[n, 1], e_recv.at[n, 1], on_line(onward, core)))

    for count, n in enumerate(order):
        onward, back = ways(n)
        partb[n] = dot(gated[...], w_buf[:, 512 * n : 512 * (n + 1)])
        remote(parta.at[n], recva.at[n], a_send.at[n], a_recv.at[n], on_line(x, core)).wait_recv()
        partb[n] = partb[n] + recva[n].astype(F32)
        sumb[n] = partb[n].astype(BF16)
        far = rows_of((x + 2) % NX)
        go(remote(sumb.at[n, far, :], relay.at[n], f_send.at[n], f_recv.at[n], on_line(onward, core)))
        go(remote(sumb.at[n, rows_of(back), :], recvb.at[n, 0], e_send.at[n, 0], e_recv.at[n, 0], on_line(back, core)))
        if count >= 2:
            send_on(order[count - 2])
    send_on(order[2])
    send_on(order[3])
    for n in order:
        total = partb[n, rows_of(x), :]
        for i in range(2):
            remote(
                hop.at[n], recvb.at[n, i], e_send.at[n, i], e_recv.at[n, i], on_line(x, core)
            ).wait_recv()
            total = total + recvb[n, i].astype(F32)
        out_ref[:, 512 * n : 512 * (n + 1)] = total.astype(BF16)

    for copy in sends:
        copy.wait_send()
    for h in range(NH):

        @pl.when(z != 2 * h + core)
        def _():
            remote(msg.at[h], parts.at[z], m_send.at[h], m_recv.at[z], owner(h)).wait_send()

    @pl.when(owns)
    def _():
        for j in range(NZ):

            @pl.when(j != z)
            def _():
                remote(xst.at[j], xin.at[mine], x_send.at[j], x_recv.at[mine], at(y, j)).wait_send()

        for i in range(1, NY):

            @pl.when(y + i < NY)
            def _():
                remote(rmsg, rowbuf.at[y], r_send.at[i - 1], r_recv.at[y], at((y + i) % NY, z)).wait_send()


def on_device(query, keys, values, gate_logit, beta_logit, decay_rate, norm_gain, gate_z, out_weight):
    hbm = pl.BlockSpec(memory_space=pltpu.HBM)
    dma = pltpu.SemaphoreType.DMA
    pairs = NB * NH
    scratch = [
        pltpu.VMEM((512, 256), BF16),
        pltpu.VMEM((512, 256), BF16),
        pltpu.VMEM((512, 512), BF16),
        pltpu.VMEM((NH, 512), F32),
        pltpu.VMEM((NH, 512), F32),
        pltpu.VMEM((1, NH), F32),
        pltpu.VMEM((1, BLK), F32),
        pltpu.VMEM((512, 512), BF16),
        pltpu.VMEM((512, 2048), BF16),
        pltpu.VMEM((16, BLK), F32),
        pltpu.VMEM((NB, 32, BLK), F32),
        pltpu.VMEM((NB, BLK, 32), F32),
        pltpu.VMEM((2, 512, 1), F32),
        pltpu.VMEM((2 * NB, BLK, BLK), BF16),
        pltpu.VMEM((pairs, BLK, BLK), BF16),
        pltpu.VMEM((8, BLK, BLK), F32),
        pltpu.VMEM((8, BLK, BLK), F32),
        pltpu.VMEM((pairs, BLK, BLK), F32),
        pltpu.VMEM((pairs, BLK, BLK), BF16),
        pltpu.VMEM((NH, BLK, 2 * BLK), F32),
        pltpu.VMEM((pairs, BLK, 2 * BLK), BF16),
        pltpu.VMEM((pairs, BLK, 2 * BLK), BF16),
        pltpu.VMEM((NH, BLK, 2 * BLK), BF16),
        pltpu.VMEM((NH, ROWS_M, BLK), BF16),
        pltpu.VMEM((NH, 512, BLK), F32),
        pltpu.VMEM((NH, 512, BLK), BF16),
        pltpu.VMEM((512, 512), F32),
        pltpu.VMEM((14, ROWS_M, BLK), BF16),
        pltpu.VMEM((ROWS_M, BLK), BF16),
        pltpu.VMEM((NY, ROWS_M, BLK), BF16),
        pltpu.VMEM((BLK, BLK), F32),
        pltpu.VMEM((NZ, BLK, BLK), BF16),
        pltpu.VMEM((NH, BLK, BLK), BF16),
        pltpu.VMEM((256, 512), BF16),
        pltpu.VMEM((4, 256, 512), BF16),
        pltpu.VMEM((4, 256, 512), BF16),
        pltpu.VMEM((4, 256, 512), F32),
        pltpu.VMEM((4, 256, 512), BF16),
        pltpu.VMEM((4, 64, 512), BF16),
        pltpu.VMEM((4, 64, 512), BF16),
        pltpu.VMEM((4, 2, 64, 512), BF16),
        dma((9,)),
        dma((4,)), dma((8,)),
        dma((3,)), dma((4,)),
        dma((8,)), dma((4,)),
        dma((4,)), dma((4,)),
        dma((4,)), dma((4,)),
        dma((4, 2)), dma((4, 2)),
    ]
    return pl.pallas_call(
        kernel,
        out_shape=jax.ShapeDtypeStruct((64, 2048), BF16),
        in_specs=[hbm] * 9,
        out_specs=pl.BlockSpec(memory_space=pltpu.VMEM),
        scratch_shapes=scratch,
        compiler_params=pltpu.CompilerParams(
            collective_id=0, has_side_effects=True, vmem_limit_bytes=48 * 1024 * 1024
        ),
    )(
        query, keys, values, gate_logit.T, beta_logit.T, decay_rate.reshape(1, NH),
        norm_gain.reshape(1, BLK), gate_z, out_weight,
    )


def solution(mesh):
    return jax.shard_map(
        on_device,
        mesh=mesh,
        in_specs=(
            P("seq", "head"),
            P("seq", "head"),
            P("seq", "head"),
            P("seq", "head"),
            P("seq", "head"),
            P("head"),
            P(),
            P("seq", "head"),
            P("head", None),
        ),
        out_specs=P(("seq", "head"), None),
        check_vma=False,
    )
```

```python
import jax
import jax.numpy as jnp
from jax import lax
from jax.experimental import pallas as pl
from jax.experimental.pallas import tpu as pltpu
from jax.sharding import PartitionSpec as P

BLK = 128
NB = 4
NH = 4
NY = 4
NZ = 8
NX = 4
ROWS_D = 128
ROWS_C = 144
ROWS_M = 272
PREFIXES = ((8, 2, 14), (12, 4, 15), (12, 10, 16), (16, 6, 17))
BEFORE = (None, 0, 8, 14, 12, 15, 16, 17)
F32 = jnp.float32
BF16 = jnp.bfloat16


def dot(left, right):
    return jnp.dot(left, right, preferred_element_type=F32)


def dot_nt(left, right):
    return lax.dot_general(left, right, (((1,), (1,)), ((), ())), preferred_element_type=F32)


def split3(x):
    hi = x.astype(BF16)
    rest = x - hi.astype(F32)
    mid = rest.astype(BF16)
    low = (rest - mid.astype(F32)).astype(BF16)
    return hi, mid, low


def softplus(x):
    y = jnp.exp(-jnp.abs(x))
    small = y * (1.0 - y * (0.5 - y * (1.0 / 3.0 - y * 0.25)))
    return jnp.maximum(x, 0.0) + jnp.where(y < 0.01, small, jnp.log(1.0 + y))


def sigmoid(x):
    return 1.0 / (1.0 + jnp.exp(-x))


def gates(gl_ref, bl_ref, rate_ref, k_ref, q_ref, s):
    same = lax.broadcasted_iota(jnp.int32, (NH, NH), 0) == lax.broadcasted_iota(jnp.int32, (NH, NH), 1)
    rate = jnp.sum(jnp.where(same, rate_ref[...], 0.0), axis=1, keepdims=True)
    g4 = -rate * softplus(gl_ref[...])
    beta4 = sigmoid(bl_ref[...])
    for b in range(NB):
        s["g16"][pl.ds(4 * b, 4), :] = g4[:, BLK * b : BLK * (b + 1)]
    row_ids = lax.broadcasted_iota(jnp.int32, (BLK, BLK), 0)
    col_ids = lax.broadcasted_iota(jnp.int32, (BLK, BLK), 1)
    upper = jnp.where(row_ids <= col_ids, 1.0, 0.0).astype(BF16)
    hi, mid, low = split3(s["g16"][...])
    s["g16"][...] = dot(hi, upper) + dot(mid, upper) + dot(low, upper)
    for b in range(NB):
        for kh in range(2):
            kf = k_ref[pl.ds(BLK * b, BLK), BLK * kh : BLK * (kh + 1)].astype(F32)
            kt = kf.T
            s["kt"][2 * b + kh] = kt.astype(BF16)
            rk = lax.rsqrt(jnp.sum(kt * kt, axis=0, keepdims=True) + 1e-06)
            s["rows"][b, pl.ds(24 + 2 * kh, 1), :] = rk
            s["rows"][b, pl.ds(25 + 2 * kh, 1), :] = rk
            qf = q_ref[pl.ds(BLK * b, BLK), BLK * kh : BLK * (kh + 1)].astype(F32)
            s["rq"][kh, pl.ds(BLK * b, BLK), :] = lax.rsqrt(
                jnp.sum(qf * qf, axis=1, keepdims=True) + 1e-06
            )
        c = s["g16"][pl.ds(4 * b, 4), :]
        beta = beta4[:, BLK * b : BLK * (b + 1)]
        rk4 = s["rows"][b, pl.ds(24, 4), :]
        end = c[:, BLK - 1 : BLK]
        ec = jnp.exp(c)
        s["rows"][b, pl.ds(0, 4), :] = c
        s["rows"][b, pl.ds(4, 4), :] = beta * rk4
        s["rows"][b, pl.ds(8, 4), :] = rk4 * jnp.exp(end - c)
        s["rows"][b, pl.ds(12, 4), :] = ec
        s["rows"][b, pl.ds(16, 4), :] = beta
        s["rows"][b, pl.ds(20, 4), :] = beta * rk4 * ec
        s["rows"][b, pl.ds(28, 4), :] = jnp.exp(jnp.broadcast_to(end, (4, BLK)))
        s["cols"][b] = s["rows"][b].T


def block_terms(kh, k_ref, q_ref, v_ref, s):
    row_ids = lax.broadcasted_iota(jnp.int32, (BLK, BLK), 0)
    col_ids = lax.broadcasted_iota(jnp.int32, (BLK, BLK), 1)
    inclusive = col_ids <= row_ids
    differ = row_ids ^ col_ids
    ident = jnp.where(row_ids == col_ids, 1.0, 0.0)
    key_lanes = slice(BLK * kh, BLK * (kh + 1))
    pairs = [(b, h) for b in range(NB) for h in (2 * kh, 2 * kh + 1)]
    for b in range(NB):
        tok = pl.ds(b * BLK, BLK)
        cols = s["cols"][b]
        kt = s["kt"][2 * b + kh]
        kk = dot(k_ref[tok, key_lanes], kt)
        qk = dot(q_ref[tok, key_lanes], kt)
        rk = s["rows"][b, pl.ds(24 + 2 * kh, 1), :]
        for h in (2 * kh, 2 * kh + 1):
            gap = cols[:, h : h + 1] - s["rows"][b, pl.ds(h, 1), :]
            ratio = jnp.exp(jnp.where(inclusive, gap, -1e30)) * rk
            s["mix"][4 * b + h] = (ratio * qk).astype(BF16)
            low = cols[:, 4 + h : 5 + h] * ratio * kk
            s["low"][2 * b + h % 2] = low
            s["inv"][2 * b + h % 2] = ident - jnp.where(differ == 1, low, 0.0)
    for level in range(1, 7):
        here = (differ >> level) == 1
        part = {}
        for b, h in pairs:
            n = 2 * b + h % 2
            off = jnp.where(here, s["low"][n], 0.0).astype(BF16)
            part[n] = dot(off, s["inv"][n].astype(BF16)).astype(BF16)
        for b, h in pairs:
            n = 2 * b + h % 2
            inv = s["inv"][n]
            s["inv"][n] = inv - dot(inv.astype(BF16), part[n])
    for b, h in pairs:
        tok = pl.ds(b * BLK, BLK)
        inv = s["inv"][2 * b + h % 2]
        t_v = (inv * s["rows"][b, pl.ds(16 + h, 1), :]).astype(BF16)
        t_k = (inv * s["rows"][b, pl.ds(20 + h, 1), :]).astype(BF16)
        s["upd"][4 * b + h] = dot(t_v, v_ref[tok, BLK * h : BLK * (h + 1)])
        s["wts"][4 * b + h] = dot(t_k, k_ref[tok, key_lanes]).astype(BF16)


def run_shard(kh, s):
    heads = (2 * kh, 2 * kh + 1)
    row_ids = lax.broadcasted_iota(jnp.int32, (BLK, 2 * BLK), 0)
    col_ids = lax.broadcasted_iota(jnp.int32, (BLK, 2 * BLK), 1)
    states = {h: jnp.where(row_ids + BLK == col_ids, 1.0, 0.0) for h in heads}
    for b in range(NB):
        cols = s["cols"][b]
        for h in heads:
            n = 4 * b + h
            state = states[h].astype(BF16)
            s["sb"][n] = state
            ws = dot(s["wts"][n], state)
            res_s = s["upd"][n] - ws[:, :BLK]
            res_a = -ws[:, BLK:]
            end = cols[:, 8 + h : 9 + h]
            s["rb"][n, :, :BLK] = res_s.astype(BF16)
            s["rb"][n, :, BLK:] = res_a.astype(BF16)
            s["re"][h, :, :BLK] = (end * res_s).astype(BF16)
            s["re"][h, :, BLK:] = (end * res_a).astype(BF16)
        for h in heads:
            gain = s["rows"][b, pl.ds(28 + h, 1), :]
            grow = dot(s["kt"][2 * b + kh], s["re"][h])
            states[h] = jnp.concatenate([gain, gain], axis=1) * states[h] + grow
    return states


def write_message(ref, c, fix, inject):
    c_ids = lax.broadcasted_iota(jnp.int32, (16, BLK), 0)
    hi, mid, low = (part.astype(F32) for part in split3(jnp.broadcast_to(c, (16, BLK))))
    terms = jnp.where(c_ids == 0, hi, jnp.where(c_ids == 1, mid, jnp.where(c_ids == 2, low, 0.0)))
    ref[:ROWS_D, :] = fix.astype(BF16)
    ref[ROWS_D:ROWS_C, :] = terms.astype(BF16)
    ref[ROWS_C:, :] = inject.astype(BF16)


def decay_of(ref):
    return jnp.sum(ref[ROWS_D:ROWS_C, :].astype(F32), axis=0, keepdims=True)


def compose(first, second, out):
    c_1, c_2 = decay_of(first), decay_of(second)
    prod = dot(first[...], second[:ROWS_D, :])
    fix = c_2 * first[:ROWS_D, :].astype(F32) + c_1 * second[:ROWS_D, :].astype(F32) - prod[:ROWS_D]
    inject = c_2 * first[ROWS_C:, :].astype(F32) + second[ROWS_C:, :].astype(F32) - prod[ROWS_C:]
    write_message(out, c_1 * c_2, fix, inject)


def step(ref, state):
    moved = decay_of(ref) * state - dot(state.astype(BF16), ref[:ROWS_D, :])
    return moved + ref[ROWS_C:, :].astype(F32)


def block_output(b, q_ref, s):
    tok = pl.ds(b * BLK, BLK)
    for h in range(NH):
        n = 4 * b + h
        kh = h // 2
        qs = dot(q_ref[tok, BLK * kh : BLK * (kh + 1)], s["sb"][n])
        out = s["cols"][b, :, 12 + h : 13 + h] * qs + dot(s["mix"][n], s["rb"][n])
        s["oloc"][h, tok, :] = out[:, :BLK]
        s["corr"][h, tok, :] = out[:, BLK:].astype(BF16)


def kernel(
    q_hbm, k_hbm, v_hbm, gl_hbm, bl_hbm, rate_hbm, gain_hbm, z_hbm, w_hbm, out_ref,
    q_ref, k_ref, v_ref, gl_ref, bl_ref, rate_ref, gain_ref, z_buf, w_buf,
    g16, rows, cols, rq, kt, mix, low, inv, upd, wts, sb, rb, re, msg, oloc, corr,
    gate, parts, rmsg, rowbuf, start, xst, xin,
    gated, parta, recva, partb, sumb, relay, hop, recvb,
    load_sem, m_send, m_recv, r_send, r_recv, x_send, x_recv,
    a_send, a_recv, f_send, f_recv, e_send, e_recv,
):
    s = dict(
        g16=g16, rows=rows, cols=cols, rq=rq, kt=kt, mix=mix, low=low, inv=inv, upd=upd, wts=wts,
        sb=sb, rb=rb, re=re, msg=msg, oloc=oloc, corr=corr,
    )
    loads = [
        pltpu.make_async_copy(src, dst, load_sem.at[i])
        for i, (src, dst) in enumerate([
            (gl_hbm, gl_ref), (bl_hbm, bl_ref), (rate_hbm, rate_ref), (k_hbm, k_ref), (q_hbm, q_ref),
            (v_hbm, v_ref), (gain_hbm, gain_ref), (z_hbm, z_buf), (w_hbm, w_buf),
        ])
    ]
    for load in loads:
        load.start()
    seq = lax.axis_index("seq")
    head = lax.axis_index("head")
    y, z = seq // NZ, seq % NZ
    x, core = head // 2, head % 2
    mine = z // 2
    owns = z % 2 == core

    def at(y_to, z_to):
        return (y_to * NZ + z_to, head)

    def owner(h):
        return at(y, 2 * h + core)

    def on_line(x_to, core_to):
        return (seq, 2 * x_to + core_to)

    def remote(src, dst, send, recv, device):
        return pltpu.make_async_remote_copy(
            src_ref=src, dst_ref=dst, send_sem=send, recv_sem=recv,
            device_id=device, device_id_type=pl.DeviceIdType.MESH,
        )

    ahead, behind = (x + 1) % NX, (x + NX - 1) % NX
    peers = [at(y, (z + i) % NZ) for i in range(1, NZ)]
    peers += [at((y + i) % NY, z) for i in range(1, NY)]
    peers += [on_line(ahead, core), on_line(behind, core), on_line(x, 1 - core)]
    barrier = pltpu.get_barrier_semaphore()
    for peer in peers:
        pl.semaphore_signal(barrier, inc=1, device_id=peer, device_id_type=pl.DeviceIdType.MESH)
    for load in loads[:6]:
        load.wait()

    gates(gl_ref, bl_ref, rate_ref, k_ref, q_ref, s)
    sends = []

    def go(copy):
        copy.start()
        sends.append(copy)

    row_ids = lax.broadcasted_iota(jnp.int32, (BLK, BLK), 0)
    eye = row_ids == lax.broadcasted_iota(jnp.int32, (BLK, BLK), 1)
    for kh in range(2):
        block_terms(kh, k_ref, q_ref, v_ref, s)
        states = run_shard(kh, s)
        if kh == 0:
            pl.semaphore_wait(barrier, len(peers))
        for h in (2 * kh, 2 * kh + 1):
            total = g16[pl.ds(h, 1), :]
            for b in range(1, NB):
                total = total + g16[pl.ds(4 * b + h, 1), :]
            c = jnp.exp(jnp.broadcast_to(total[:, BLK - 1 : BLK], (1, BLK)))
            fix = jnp.where(eye, c, 0.0) - states[h][:, BLK:]
            write_message(msg.at[h], c, fix.T, states[h][:, :BLK].T)

            @pl.when(z != 2 * h + core)
            def _():
                remote(msg.at[h], parts.at[z], m_send.at[h], m_recv.at[z], owner(h)).start()

            @pl.when(z == 2 * h + core)
            def _():
                parts[z] = msg[h]

    for b in range(NB):
        block_output(b, q_ref, s)
    for load in loads[6:]:
        load.wait()
    zf = z_buf[...].astype(F32)
    zs = zf * sigmoid(zf)
    for h in range(NH):
        gate[:, BLK * h : BLK * (h + 1)] = zs[:, BLK * h : BLK * (h + 1)] * gain_ref[...]

    @pl.when(owns)
    def _():
        for k in range(4):
            for j in (2 * k, 2 * k + 1):

                @pl.when(z != j)
                def _():
                    remote(msg.at[0], parts.at[j], m_send.at[0], m_recv.at[j], at(y, z)).wait_recv()

            compose(parts.at[2 * k], parts.at[2 * k + 1], parts.at[8 + k])
        for k in range(2):
            compose(parts.at[8 + 2 * k], parts.at[9 + 2 * k], parts.at[12 + k])
        compose(parts.at[12], parts.at[13], rmsg)
        for i in range(NY - 1, 0, -1):

            @pl.when(y + i < NY)
            def _():
                remote(rmsg, rowbuf.at[y], r_send.at[i - 1], r_recv.at[y], at((y + i) % NY, z)).start()

        for first, second, out in PREFIXES:
            compose(parts.at[first], parts.at[second], parts.at[out])
        start[...] = jnp.zeros_like(start)
        for r in range(NY - 1):

            @pl.when(r < y)
            def _():
                remote(rmsg, rowbuf.at[r], r_send.at[0], r_recv.at[r], at(y, z)).wait_recv()
                if r == 0:
                    start[...] = rowbuf[r, ROWS_C:, :].astype(F32)
                else:
                    start[...] = step(rowbuf.at[r], start[...])

        row_state = start[...]
        for j, stretch in enumerate(BEFORE):
            at_shard = row_state if stretch is None else step(parts.at[stretch], row_state)
            xst[j] = at_shard.astype(BF16)

            @pl.when(j != z)
            def _():
                remote(xst.at[j], xin.at[mine], x_send.at[j], x_recv.at[mine], at(y, j)).start()

            @pl.when(j == z)
            def _():
                xin[mine] = xst[j]

    for h in range(NH):

        @pl.when(z != 2 * h + core)
        def _():
            remote(xst.at[0], xin.at[h], x_send.at[0], x_recv.at[h], at(y, z)).wait_recv()

    def gate_half(which):
        for h in range(NH):
            for j in range(NX):
                tok = pl.ds(pl.multiple_of((2 * j + which) * 64, 64), 64)
                core_out = oloc[h, tok, :] + dot_nt(corr[h, tok, :], xin[h])
                r = rq[h // 2, tok, :]
                mean = jnp.mean(core_out * core_out, axis=1, keepdims=True)
                scale = r * lax.rsqrt(r * r * mean + 1e-06)
                lanes = slice(BLK * h, BLK * (h + 1))
                gated[64 * j : 64 * (j + 1), lanes] = (core_out * scale * gate[tok, lanes]).astype(BF16)

    order = (0, 2, 1, 3)
    gate_half(1 - core)
    for n in order:
        parta[n] = dot(gated[...], w_buf[:, 512 * n : 512 * (n + 1)]).astype(BF16)
        go(remote(parta.at[n], recva.at[n], a_send.at[n], a_recv.at[n], on_line(x, 1 - core)))
    gate_half(core)

    def rows_of(chip):
        return pl.ds(pl.multiple_of(64 * chip, 64), 64)

    def ways(n):
        return (ahead, behind) if n < 2 else (behind, ahead)

    def send_on(n):
        onward, back = ways(n)
        remote(sumb.at[n, rows_of(x), :], relay.at[n], f_send.at[n], f_recv.at[n], on_line(x, core)).wait_recv()
        hop[n] = (partb[n, rows_of(onward), :] + relay[n].astype(F32)).astype(BF16)
        go(remote(hop.at[n], recvb.at[n, 1], e_send.at[n, 1], e_recv.at[n, 1], on_line(onward, core)))

    for count, n in enumerate(order):
        onward, back = ways(n)
        partb[n] = dot(gated[...], w_buf[:, 512 * n : 512 * (n + 1)])
        remote(parta.at[n], recva.at[n], a_send.at[n], a_recv.at[n], on_line(x, core)).wait_recv()
        partb[n] = partb[n] + recva[n].astype(F32)
        sumb[n] = partb[n].astype(BF16)
        far = rows_of((x + 2) % NX)
        go(remote(sumb.at[n, far, :], relay.at[n], f_send.at[n], f_recv.at[n], on_line(onward, core)))
        go(remote(sumb.at[n, rows_of(back), :], recvb.at[n, 0], e_send.at[n, 0], e_recv.at[n, 0], on_line(back, core)))
        if count >= 2:
            send_on(order[count - 2])
    send_on(order[2])
    send_on(order[3])
    for n in order:
        total = partb[n, rows_of(x), :]
        for i in range(2):
            remote(
                hop.at[n], recvb.at[n, i], e_send.at[n, i], e_recv.at[n, i], on_line(x, core)
            ).wait_recv()
            total = total + recvb[n, i].astype(F32)
        out_ref[:, 512 * n : 512 * (n + 1)] = total.astype(BF16)

    for copy in sends:
        copy.wait_send()
    for h in range(NH):

        @pl.when(z != 2 * h + core)
        def _():
            remote(msg.at[h], parts.at[z], m_send.at[h], m_recv.at[z], owner(h)).wait_send()

    @pl.when(owns)
    def _():
        for j in range(NZ):

            @pl.when(j != z)
            def _():
                remote(xst.at[j], xin.at[mine], x_send.at[j], x_recv.at[mine], at(y, j)).wait_send()

        for i in range(1, NY):

            @pl.when(y + i < NY)
            def _():
                remote(rmsg, rowbuf.at[y], r_send.at[i - 1], r_recv.at[y], at((y + i) % NY, z)).wait_send()


def on_device(query, keys, values, gate_logit, beta_logit, decay_rate, norm_gain, gate_z, out_weight):
    hbm = pl.BlockSpec(memory_space=pltpu.HBM)
    dma = pltpu.SemaphoreType.DMA
    pairs = NB * NH
    scratch = [
        pltpu.VMEM((512, 256), BF16),
        pltpu.VMEM((512, 256), BF16),
        pltpu.VMEM((512, 512), BF16),
        pltpu.VMEM((NH, 512), F32),
        pltpu.VMEM((NH, 512), F32),
        pltpu.VMEM((1, NH), F32),
        pltpu.VMEM((1, BLK), F32),
        pltpu.VMEM((512, 512), BF16),
        pltpu.VMEM((512, 2048), BF16),
        pltpu.VMEM((16, BLK), F32),
        pltpu.VMEM((NB, 32, BLK), F32),
        pltpu.VMEM((NB, BLK, 32), F32),
        pltpu.VMEM((2, 512, 1), F32),
        pltpu.VMEM((2 * NB, BLK, BLK), BF16),
        pltpu.VMEM((pairs, BLK, BLK), BF16),
        pltpu.VMEM((8, BLK, BLK), F32),
        pltpu.VMEM((8, BLK, BLK), F32),
        pltpu.VMEM((pairs, BLK, BLK), F32),
        pltpu.VMEM((pairs, BLK, BLK), BF16),
        pltpu.VMEM((pairs, BLK, 2 * BLK), BF16),
        pltpu.VMEM((pairs, BLK, 2 * BLK), BF16),
        pltpu.VMEM((NH, BLK, 2 * BLK), BF16),
        pltpu.VMEM((NH, ROWS_M, BLK), BF16),
        pltpu.VMEM((NH, 512, BLK), F32),
        pltpu.VMEM((NH, 512, BLK), BF16),
        pltpu.VMEM((512, 512), F32),
        pltpu.VMEM((18, ROWS_M, BLK), BF16),
        pltpu.VMEM((ROWS_M, BLK), BF16),
        pltpu.VMEM((NY, ROWS_M, BLK), BF16),
        pltpu.VMEM((BLK, BLK), F32),
        pltpu.VMEM((NZ, BLK, BLK), BF16),
        pltpu.VMEM((NH, BLK, BLK), BF16),
        pltpu.VMEM((256, 512), BF16),
        pltpu.VMEM((4, 256, 512), BF16),
        pltpu.VMEM((4, 256, 512), BF16),
        pltpu.VMEM((4, 256, 512), F32),
        pltpu.VMEM((4, 256, 512), BF16),
        pltpu.VMEM((4, 64, 512), BF16),
        pltpu.VMEM((4, 64, 512), BF16),
        pltpu.VMEM((4, 2, 64, 512), BF16),
        dma((9,)),
        dma((4,)), dma((8,)),
        dma((3,)), dma((4,)),
        dma((8,)), dma((4,)),
        dma((4,)), dma((4,)),
        dma((4,)), dma((4,)),
        dma((4, 2)), dma((4, 2)),
    ]
    return pl.pallas_call(
        kernel,
        out_shape=jax.ShapeDtypeStruct((64, 2048), BF16),
        in_specs=[hbm] * 9,
        out_specs=pl.BlockSpec(memory_space=pltpu.VMEM),
        scratch_shapes=scratch,
        compiler_params=pltpu.CompilerParams(
            collective_id=0, has_side_effects=True, vmem_limit_bytes=56 * 1024 * 1024
        ),
    )(
        query, keys, values, gate_logit.T, beta_logit.T, decay_rate.reshape(1, NH),
        norm_gain.reshape(1, BLK), gate_z, out_weight,
    )


def solution(mesh):
    return jax.shard_map(
        on_device,
        mesh=mesh,
        in_specs=(
            P("seq", "head"),
            P("seq", "head"),
            P("seq", "head"),
            P("seq", "head"),
            P("seq", "head"),
            P("head"),
            P(),
            P("seq", "head"),
            P("head", None),
        ),
        out_specs=P(("seq", "head"), None),
        check_vma=False,
    )
```

```python
import jax
import jax.numpy as jnp
from jax import lax
from jax.experimental import pallas as pl
from jax.experimental.pallas import tpu as pltpu
from jax.sharding import PartitionSpec as P

BLK = 128
NB = 4
NH = 4
NY = 4
NZ = 8
NX = 4
ROWS_D = 128
ROWS_C = 144
ROWS_M = 272
PREFIXES = ((8, 2, 14), (12, 4, 15), (12, 10, 16), (16, 6, 17))
BEFORE = (None, 0, 8, 14, 12, 15, 16, 17)
F32 = jnp.float32
BF16 = jnp.bfloat16


def dot(left, right):
    return jnp.dot(left, right, preferred_element_type=F32)


def dot_nt(left, right):
    return lax.dot_general(left, right, (((1,), (1,)), ((), ())), preferred_element_type=F32)


def split3(x):
    hi = x.astype(BF16)
    rest = x - hi.astype(F32)
    mid = rest.astype(BF16)
    low = (rest - mid.astype(F32)).astype(BF16)
    return hi, mid, low


def softplus(x):
    y = jnp.exp(-jnp.abs(x))
    small = y * (1.0 - y * (0.5 - y * (1.0 / 3.0 - y * 0.25)))
    return jnp.maximum(x, 0.0) + jnp.where(y < 0.01, small, jnp.log(1.0 + y))


def sigmoid(x):
    return 1.0 / (1.0 + jnp.exp(-x))


def gates(gl_ref, bl_ref, rate_ref, k_ref, q_ref, s):
    same = lax.broadcasted_iota(jnp.int32, (NH, NH), 0) == lax.broadcasted_iota(jnp.int32, (NH, NH), 1)
    rate = jnp.sum(jnp.where(same, rate_ref[...], 0.0), axis=1, keepdims=True)
    g4 = -rate * softplus(gl_ref[...])
    beta4 = sigmoid(bl_ref[...])
    for b in range(NB):
        s["g16"][pl.ds(4 * b, 4), :] = g4[:, BLK * b : BLK * (b + 1)]
    row_ids = lax.broadcasted_iota(jnp.int32, (BLK, BLK), 0)
    col_ids = lax.broadcasted_iota(jnp.int32, (BLK, BLK), 1)
    upper = jnp.where(row_ids <= col_ids, 1.0, 0.0).astype(BF16)
    hi, mid, low = split3(s["g16"][...])
    s["g16"][...] = dot(hi, upper) + dot(mid, upper) + dot(low, upper)
    for b in range(NB):
        for kh in range(2):
            kf = k_ref[pl.ds(BLK * b, BLK), BLK * kh : BLK * (kh + 1)].astype(F32)
            kt = kf.T
            s["kt"][2 * b + kh] = kt.astype(BF16)
            rk = lax.rsqrt(jnp.sum(kt * kt, axis=0, keepdims=True) + 1e-06)
            s["rows"][b, pl.ds(24 + 2 * kh, 1), :] = rk
            s["rows"][b, pl.ds(25 + 2 * kh, 1), :] = rk
            qf = q_ref[pl.ds(BLK * b, BLK), BLK * kh : BLK * (kh + 1)].astype(F32)
            s["rq"][kh, pl.ds(BLK * b, BLK), :] = lax.rsqrt(
                jnp.sum(qf * qf, axis=1, keepdims=True) + 1e-06
            )
        c = s["g16"][pl.ds(4 * b, 4), :]
        beta = beta4[:, BLK * b : BLK * (b + 1)]
        rk4 = s["rows"][b, pl.ds(24, 4), :]
        end = c[:, BLK - 1 : BLK]
        ec = jnp.exp(c)
        s["rows"][b, pl.ds(0, 4), :] = c
        s["rows"][b, pl.ds(4, 4), :] = beta * rk4
        s["rows"][b, pl.ds(8, 4), :] = rk4 * jnp.exp(end - c)
        s["rows"][b, pl.ds(12, 4), :] = ec
        s["rows"][b, pl.ds(16, 4), :] = beta
        s["rows"][b, pl.ds(20, 4), :] = beta * rk4 * ec
        s["rows"][b, pl.ds(28, 4), :] = jnp.exp(jnp.broadcast_to(end, (4, BLK)))
        s["cols"][b] = s["rows"][b].T


def block_terms(kh, k_ref, q_ref, v_ref, s):
    row_ids = lax.broadcasted_iota(jnp.int32, (BLK, BLK), 0)
    col_ids = lax.broadcasted_iota(jnp.int32, (BLK, BLK), 1)
    inclusive = col_ids <= row_ids
    differ = row_ids ^ col_ids
    ident = jnp.where(row_ids == col_ids, 1.0, 0.0)
    key_lanes = slice(BLK * kh, BLK * (kh + 1))
    pairs = [(b, h) for b in range(NB) for h in (2 * kh, 2 * kh + 1)]
    for b in range(NB):
        tok = pl.ds(b * BLK, BLK)
        cols = s["cols"][b]
        kt = s["kt"][2 * b + kh]
        kk = dot(k_ref[tok, key_lanes], kt)
        qk = dot(q_ref[tok, key_lanes], kt)
        rk = s["rows"][b, pl.ds(24 + 2 * kh, 1), :]
        for h in (2 * kh, 2 * kh + 1):
            gap = cols[:, h : h + 1] - s["rows"][b, pl.ds(h, 1), :]
            ratio = jnp.exp(jnp.where(inclusive, gap, -1e30)) * rk
            s["mix"][4 * b + h] = (ratio * qk).astype(BF16)
            low = cols[:, 4 + h : 5 + h] * ratio * kk
            s["low"][2 * b + h % 2] = low
            s["inv"][2 * b + h % 2] = ident - jnp.where(differ == 1, low, 0.0)
        yield
    for level in range(1, 7):
        here = (differ >> level) == 1
        part = {}
        for b, h in pairs:
            n = 2 * b + h % 2
            off = jnp.where(here, s["low"][n], 0.0).astype(BF16)
            part[n] = dot(off, s["inv"][n].astype(BF16)).astype(BF16)
        yield
        for b, h in pairs:
            n = 2 * b + h % 2
            inv = s["inv"][n]
            s["inv"][n] = inv - dot(inv.astype(BF16), part[n])
        yield
    for b, h in pairs:
        tok = pl.ds(b * BLK, BLK)
        inv = s["inv"][2 * b + h % 2]
        t_v = (inv * s["rows"][b, pl.ds(16 + h, 1), :]).astype(BF16)
        t_k = (inv * s["rows"][b, pl.ds(20 + h, 1), :]).astype(BF16)
        s["upd"][4 * b + h] = dot(t_v, v_ref[tok, BLK * h : BLK * (h + 1)])
        s["wts"][4 * b + h] = dot(t_k, k_ref[tok, key_lanes]).astype(BF16)


def run_shard(kh, states, s):
    heads = (2 * kh, 2 * kh + 1)
    row_ids = lax.broadcasted_iota(jnp.int32, (BLK, 2 * BLK), 0)
    col_ids = lax.broadcasted_iota(jnp.int32, (BLK, 2 * BLK), 1)
    for h in heads:
        states[h] = jnp.where(row_ids + BLK == col_ids, 1.0, 0.0)
    for b in range(NB):
        cols = s["cols"][b]
        for h in heads:
            n = 4 * b + h
            state = states[h].astype(BF16)
            s["sb"][n] = state
            ws = dot(s["wts"][n], state)
            res_s = s["upd"][n] - ws[:, :BLK]
            res_a = -ws[:, BLK:]
            end = cols[:, 8 + h : 9 + h]
            s["rb"][n, :, :BLK] = res_s.astype(BF16)
            s["rb"][n, :, BLK:] = res_a.astype(BF16)
            s["re"][h, :, :BLK] = (end * res_s).astype(BF16)
            s["re"][h, :, BLK:] = (end * res_a).astype(BF16)
        yield
        for h in heads:
            gain = s["rows"][b, pl.ds(28 + h, 1), :]
            grow = dot(s["kt"][2 * b + kh], s["re"][h])
            states[h] = jnp.concatenate([gain, gain], axis=1) * states[h] + grow
        yield


def write_message(ref, c, fix, inject):
    c_ids = lax.broadcasted_iota(jnp.int32, (16, BLK), 0)
    hi, mid, low = (part.astype(F32) for part in split3(jnp.broadcast_to(c, (16, BLK))))
    terms = jnp.where(c_ids == 0, hi, jnp.where(c_ids == 1, mid, jnp.where(c_ids == 2, low, 0.0)))
    ref[:ROWS_D, :] = fix.astype(BF16)
    ref[ROWS_D:ROWS_C, :] = terms.astype(BF16)
    ref[ROWS_C:, :] = inject.astype(BF16)


def decay_of(ref):
    return jnp.sum(ref[ROWS_D:ROWS_C, :].astype(F32), axis=0, keepdims=True)


def compose(first, second, out):
    c_1, c_2 = decay_of(first), decay_of(second)
    prod = dot(first[...], second[:ROWS_D, :])
    fix = c_2 * first[:ROWS_D, :].astype(F32) + c_1 * second[:ROWS_D, :].astype(F32) - prod[:ROWS_D]
    inject = c_2 * first[ROWS_C:, :].astype(F32) + second[ROWS_C:, :].astype(F32) - prod[ROWS_C:]
    write_message(out, c_1 * c_2, fix, inject)


def step(ref, state):
    moved = decay_of(ref) * state - dot(state.astype(BF16), ref[:ROWS_D, :])
    return moved + ref[ROWS_C:, :].astype(F32)


def block_output(b, q_ref, s):
    tok = pl.ds(b * BLK, BLK)
    for h in range(NH):
        n = 4 * b + h
        kh = h // 2
        qs = dot(q_ref[tok, BLK * kh : BLK * (kh + 1)], s["sb"][n])
        out = s["cols"][b, :, 12 + h : 13 + h] * qs + dot(s["mix"][n], s["rb"][n])
        s["oloc"][h, tok, :] = out[:, :BLK]
        s["corr"][h, tok, :] = out[:, BLK:].astype(BF16)


def kernel(
    q_hbm, k_hbm, v_hbm, gl_hbm, bl_hbm, rate_hbm, gain_hbm, z_hbm, w_hbm, out_ref,
    q_ref, k_ref, v_ref, gl_ref, bl_ref, rate_ref, gain_ref, z_buf, w_buf,
    g16, rows, cols, rq, kt, mix, low, inv, upd, wts, sb, rb, re, msg, oloc, corr,
    gate, parts, rmsg, rowbuf, start, xst, xin,
    gated, parta, recva, partb, sumb, relay, hop, recvb,
    load_sem, m_send, m_recv, r_send, r_recv, x_send, x_recv,
    a_send, a_recv, f_send, f_recv, e_send, e_recv,
):
    s = dict(
        g16=g16, rows=rows, cols=cols, rq=rq, kt=kt, mix=mix, low=low, inv=inv, upd=upd, wts=wts,
        sb=sb, rb=rb, re=re, msg=msg, oloc=oloc, corr=corr,
    )
    loads = [
        pltpu.make_async_copy(src, dst, load_sem.at[i])
        for i, (src, dst) in enumerate([
            (gl_hbm, gl_ref), (bl_hbm, bl_ref), (rate_hbm, rate_ref), (k_hbm, k_ref), (q_hbm, q_ref),
            (v_hbm, v_ref), (gain_hbm, gain_ref), (z_hbm, z_buf), (w_hbm, w_buf),
        ])
    ]
    for load in loads:
        load.start()
    seq = lax.axis_index("seq")
    head = lax.axis_index("head")
    y, z = seq // NZ, seq % NZ
    x, core = head // 2, head % 2
    mine = z // 2
    owns = z % 2 == core

    def at(y_to, z_to):
        return (y_to * NZ + z_to, head)

    def owner(h):
        return at(y, 2 * h + core)

    def on_line(x_to, core_to):
        return (seq, 2 * x_to + core_to)

    def remote(src, dst, send, recv, device):
        return pltpu.make_async_remote_copy(
            src_ref=src, dst_ref=dst, send_sem=send, recv_sem=recv,
            device_id=device, device_id_type=pl.DeviceIdType.MESH,
        )

    ahead, behind = (x + 1) % NX, (x + NX - 1) % NX
    peers = [at(y, (z + i) % NZ) for i in range(1, NZ)]
    peers += [at((y + i) % NY, z) for i in range(1, NY)]
    peers += [on_line(ahead, core), on_line(behind, core), on_line(x, 1 - core)]
    barrier = pltpu.get_barrier_semaphore()
    for peer in peers:
        pl.semaphore_signal(barrier, inc=1, device_id=peer, device_id_type=pl.DeviceIdType.MESH)
    for load in loads[:6]:
        load.wait()

    gates(gl_ref, bl_ref, rate_ref, k_ref, q_ref, s)
    sends = []

    def go(copy):
        copy.start()
        sends.append(copy)

    row_ids = lax.broadcasted_iota(jnp.int32, (BLK, BLK), 0)
    eye = row_ids == lax.broadcasted_iota(jnp.int32, (BLK, BLK), 1)
    states = {}

    def send_heads(heads):
        for h in heads:
            total = g16[pl.ds(h, 1), :]
            for b in range(1, NB):
                total = total + g16[pl.ds(4 * b + h, 1), :]
            c = jnp.exp(jnp.broadcast_to(total[:, BLK - 1 : BLK], (1, BLK)))
            fix = jnp.where(eye, c, 0.0) - states[h][:, BLK:]
            write_message(msg.at[h], c, fix.T, states[h][:, :BLK].T)

            @pl.when(z != 2 * h + core)
            def _():
                remote(msg.at[h], parts.at[z], m_send.at[h], m_recv.at[z], owner(h)).start()

            @pl.when(z == 2 * h + core)
            def _():
                parts[z] = msg[h]

    for _ in block_terms(0, k_ref, q_ref, v_ref, s):
        pass
    second = block_terms(1, k_ref, q_ref, v_ref, s)
    for _ in run_shard(0, states, s):
        next(second)
    pl.semaphore_wait(barrier, len(peers))
    send_heads((0, 1))
    for _ in second:
        pass
    for _ in run_shard(1, states, s):
        pass
    send_heads((2, 3))
    for b in range(NB):
        block_output(b, q_ref, s)
    for load in loads[6:]:
        load.wait()
    zf = z_buf[...].astype(F32)
    zs = zf * sigmoid(zf)
    for h in range(NH):
        gate[:, BLK * h : BLK * (h + 1)] = zs[:, BLK * h : BLK * (h + 1)] * gain_ref[...]

    @pl.when(owns)
    def _():
        for k in range(4):
            for j in (2 * k, 2 * k + 1):

                @pl.when(z != j)
                def _():
                    remote(msg.at[0], parts.at[j], m_send.at[0], m_recv.at[j], at(y, z)).wait_recv()

            compose(parts.at[2 * k], parts.at[2 * k + 1], parts.at[8 + k])
        for k in range(2):
            compose(parts.at[8 + 2 * k], parts.at[9 + 2 * k], parts.at[12 + k])
        compose(parts.at[12], parts.at[13], rmsg)
        for i in range(NY - 1, 0, -1):

            @pl.when(y + i < NY)
            def _():
                remote(rmsg, rowbuf.at[y], r_send.at[i - 1], r_recv.at[y], at((y + i) % NY, z)).start()

        for first, second, out in PREFIXES:
            compose(parts.at[first], parts.at[second], parts.at[out])
        start[...] = jnp.zeros_like(start)
        for r in range(NY - 1):

            @pl.when(r < y)
            def _():
                remote(rmsg, rowbuf.at[r], r_send.at[0], r_recv.at[r], at(y, z)).wait_recv()
                if r == 0:
                    start[...] = rowbuf[r, ROWS_C:, :].astype(F32)
                else:
                    start[...] = step(rowbuf.at[r], start[...])

        row_state = start[...]
        for j, stretch in enumerate(BEFORE):
            at_shard = row_state if stretch is None else step(parts.at[stretch], row_state)
            xst[j] = at_shard.astype(BF16)

            @pl.when(j != z)
            def _():
                remote(xst.at[j], xin.at[mine], x_send.at[j], x_recv.at[mine], at(y, j)).start()

            @pl.when(j == z)
            def _():
                xin[mine] = xst[j]

    for h in range(NH):

        @pl.when(z != 2 * h + core)
        def _():
            remote(xst.at[0], xin.at[h], x_send.at[0], x_recv.at[h], at(y, z)).wait_recv()

    def gate_half(which, slot):
        for h in range(NH):
            for j in range(NX):
                tok = pl.ds(pl.multiple_of((2 * j + which) * 64, 64), 64)
                core_out = oloc[h, tok, :] + dot_nt(corr[h, tok, :], xin[h])
                r = rq[h // 2, tok, :]
                mean = jnp.mean(core_out * core_out, axis=1, keepdims=True)
                scale = r * lax.rsqrt(r * r * mean + 1e-06)
                lanes = slice(BLK * h, BLK * (h + 1))
                gated[slot, 64 * j : 64 * (j + 1), lanes] = (core_out * scale * gate[tok, lanes]).astype(BF16)

    order = (0, 2, 1, 3)
    def send_over(n):
        parta[n] = dot(gated[0], w_buf[:, 512 * n : 512 * (n + 1)]).astype(BF16)
        go(remote(parta.at[n], recva.at[n], a_send.at[n], a_recv.at[n], on_line(x, 1 - core)))

    gate_half(1 - core, 0)
    send_over(order[0])
    gate_half(core, 1)

    def rows_of(chip):
        return pl.ds(pl.multiple_of(64 * chip, 64), 64)

    def ways(n):
        return (ahead, behind) if n < 2 else (behind, ahead)

    def send_on(n):
        onward, back = ways(n)
        remote(sumb.at[n, rows_of(x), :], relay.at[n], f_send.at[n], f_recv.at[n], on_line(x, core)).wait_recv()
        hop[n] = (partb[n, rows_of(onward), :] + relay[n].astype(F32)).astype(BF16)
        go(remote(hop.at[n], recvb.at[n, 1], e_send.at[n, 1], e_recv.at[n, 1], on_line(onward, core)))

    for count, n in enumerate(order):
        onward, back = ways(n)
        if count < 3:
            send_over(order[count + 1])
        partb[n] = dot(gated[1], w_buf[:, 512 * n : 512 * (n + 1)])
        remote(parta.at[n], recva.at[n], a_send.at[n], a_recv.at[n], on_line(x, core)).wait_recv()
        partb[n] = partb[n] + recva[n].astype(F32)
        sumb[n] = partb[n].astype(BF16)
        far = rows_of((x + 2) % NX)
        go(remote(sumb.at[n, far, :], relay.at[n], f_send.at[n], f_recv.at[n], on_line(onward, core)))
        go(remote(sumb.at[n, rows_of(back), :], recvb.at[n, 0], e_send.at[n, 0], e_recv.at[n, 0], on_line(back, core)))
        if count >= 2:
            send_on(order[count - 2])
    send_on(order[2])
    send_on(order[3])
    for n in order:
        total = partb[n, rows_of(x), :]
        for i in range(2):
            remote(
                hop.at[n], recvb.at[n, i], e_send.at[n, i], e_recv.at[n, i], on_line(x, core)
            ).wait_recv()
            total = total + recvb[n, i].astype(F32)
        out_ref[:, 512 * n : 512 * (n + 1)] = total.astype(BF16)

    for copy in sends:
        copy.wait_send()
    for h in range(NH):

        @pl.when(z != 2 * h + core)
        def _():
            remote(msg.at[h], parts.at[z], m_send.at[h], m_recv.at[z], owner(h)).wait_send()

    @pl.when(owns)
    def _():
        for j in range(NZ):

            @pl.when(j != z)
            def _():
                remote(xst.at[j], xin.at[mine], x_send.at[j], x_recv.at[mine], at(y, j)).wait_send()

        for i in range(1, NY):

            @pl.when(y + i < NY)
            def _():
                remote(rmsg, rowbuf.at[y], r_send.at[i - 1], r_recv.at[y], at((y + i) % NY, z)).wait_send()


def on_device(query, keys, values, gate_logit, beta_logit, decay_rate, norm_gain, gate_z, out_weight):
    hbm = pl.BlockSpec(memory_space=pltpu.HBM)
    dma = pltpu.SemaphoreType.DMA
    pairs = NB * NH
    scratch = [
        pltpu.VMEM((512, 256), BF16),
        pltpu.VMEM((512, 256), BF16),
        pltpu.VMEM((512, 512), BF16),
        pltpu.VMEM((NH, 512), F32),
        pltpu.VMEM((NH, 512), F32),
        pltpu.VMEM((1, NH), F32),
        pltpu.VMEM((1, BLK), F32),
        pltpu.VMEM((512, 512), BF16),
        pltpu.VMEM((512, 2048), BF16),
        pltpu.VMEM((16, BLK), F32),
        pltpu.VMEM((NB, 32, BLK), F32),
        pltpu.VMEM((NB, BLK, 32), F32),
        pltpu.VMEM((2, 512, 1), F32),
        pltpu.VMEM((2 * NB, BLK, BLK), BF16),
        pltpu.VMEM((pairs, BLK, BLK), BF16),
        pltpu.VMEM((8, BLK, BLK), F32),
        pltpu.VMEM((8, BLK, BLK), F32),
        pltpu.VMEM((pairs, BLK, BLK), F32),
        pltpu.VMEM((pairs, BLK, BLK), BF16),
        pltpu.VMEM((pairs, BLK, 2 * BLK), BF16),
        pltpu.VMEM((pairs, BLK, 2 * BLK), BF16),
        pltpu.VMEM((NH, BLK, 2 * BLK), BF16),
        pltpu.VMEM((NH, ROWS_M, BLK), BF16),
        pltpu.VMEM((NH, 512, BLK), F32),
        pltpu.VMEM((NH, 512, BLK), BF16),
        pltpu.VMEM((512, 512), F32),
        pltpu.VMEM((18, ROWS_M, BLK), BF16),
        pltpu.VMEM((ROWS_M, BLK), BF16),
        pltpu.VMEM((NY, ROWS_M, BLK), BF16),
        pltpu.VMEM((BLK, BLK), F32),
        pltpu.VMEM((NZ, BLK, BLK), BF16),
        pltpu.VMEM((NH, BLK, BLK), BF16),
        pltpu.VMEM((2, 256, 512), BF16),
        pltpu.VMEM((4, 256, 512), BF16),
        pltpu.VMEM((4, 256, 512), BF16),
        pltpu.VMEM((4, 256, 512), F32),
        pltpu.VMEM((4, 256, 512), BF16),
        pltpu.VMEM((4, 64, 512), BF16),
        pltpu.VMEM((4, 64, 512), BF16),
        pltpu.VMEM((4, 2, 64, 512), BF16),
        dma((9,)),
        dma((4,)), dma((8,)),
        dma((3,)), dma((4,)),
        dma((8,)), dma((4,)),
        dma((4,)), dma((4,)),
        dma((4,)), dma((4,)),
        dma((4, 2)), dma((4, 2)),
    ]
    return pl.pallas_call(
        kernel,
        out_shape=jax.ShapeDtypeStruct((64, 2048), BF16),
        in_specs=[hbm] * 9,
        out_specs=pl.BlockSpec(memory_space=pltpu.VMEM),
        scratch_shapes=scratch,
        compiler_params=pltpu.CompilerParams(
            collective_id=0, has_side_effects=True, vmem_limit_bytes=56 * 1024 * 1024
        ),
    )(
        query, keys, values, gate_logit.T, beta_logit.T, decay_rate.reshape(1, NH),
        norm_gain.reshape(1, BLK), gate_z, out_weight,
    )


def solution(mesh):
    return jax.shard_map(
        on_device,
        mesh=mesh,
        in_specs=(
            P("seq", "head"),
            P("seq", "head"),
            P("seq", "head"),
            P("seq", "head"),
            P("seq", "head"),
            P("head"),
            P(),
            P("seq", "head"),
            P("head", None),
        ),
        out_specs=P(("seq", "head"), None),
        check_vma=False,
    )
```

```python
import jax
import jax.numpy as jnp
from jax import lax
from jax.experimental import pallas as pl
from jax.experimental.pallas import tpu as pltpu
from jax.sharding import PartitionSpec as P

BLK = 128
NB = 4
NH = 4
NY = 4
NZ = 8
NX = 4
ROWS_D = 128
ROWS_C = 144
ROWS_M = 272
PREFIXES = ((8, 2, 14), (12, 4, 15), (12, 10, 16), (16, 6, 17))
BEFORE = (None, 0, 8, 14, 12, 15, 16, 17)
F32 = jnp.float32
BF16 = jnp.bfloat16


def dot(left, right):
    return jnp.dot(left, right, preferred_element_type=F32)


def dot_nt(left, right):
    return lax.dot_general(left, right, (((1,), (1,)), ((), ())), preferred_element_type=F32)


def split3(x):
    hi = x.astype(BF16)
    rest = x - hi.astype(F32)
    mid = rest.astype(BF16)
    low = (rest - mid.astype(F32)).astype(BF16)
    return hi, mid, low


def softplus(x):
    y = jnp.exp(-jnp.abs(x))
    small = y * (1.0 - y * (0.5 - y * (1.0 / 3.0 - y * 0.25)))
    return jnp.maximum(x, 0.0) + jnp.where(y < 0.01, small, jnp.log(1.0 + y))


def sigmoid(x):
    return 1.0 / (1.0 + jnp.exp(-x))


def gates(gl_ref, bl_ref, rate_ref, k_ref, q_ref, s):
    same = lax.broadcasted_iota(jnp.int32, (NH, NH), 0) == lax.broadcasted_iota(jnp.int32, (NH, NH), 1)
    rate = jnp.sum(jnp.where(same, rate_ref[...], 0.0), axis=1, keepdims=True)
    g4 = -rate * softplus(gl_ref[...])
    beta4 = sigmoid(bl_ref[...])
    for b in range(NB):
        s["g16"][pl.ds(4 * b, 4), :] = g4[:, BLK * b : BLK * (b + 1)]
    row_ids = lax.broadcasted_iota(jnp.int32, (BLK, BLK), 0)
    col_ids = lax.broadcasted_iota(jnp.int32, (BLK, BLK), 1)
    upper = jnp.where(row_ids <= col_ids, 1.0, 0.0).astype(BF16)
    hi, mid, low = split3(s["g16"][...])
    s["g16"][...] = dot(hi, upper) + dot(mid, upper) + dot(low, upper)
    for b in range(NB):
        for kh in range(2):
            kf = k_ref[pl.ds(BLK * b, BLK), BLK * kh : BLK * (kh + 1)].astype(F32)
            kt = kf.T
            s["kt"][2 * b + kh] = kt.astype(BF16)
            rk = lax.rsqrt(jnp.sum(kt * kt, axis=0, keepdims=True) + 1e-06)
            s["rows"][b, pl.ds(24 + 2 * kh, 1), :] = rk
            s["rows"][b, pl.ds(25 + 2 * kh, 1), :] = rk
            qf = q_ref[pl.ds(BLK * b, BLK), BLK * kh : BLK * (kh + 1)].astype(F32)
            s["rq"][kh, pl.ds(BLK * b, BLK), :] = lax.rsqrt(
                jnp.sum(qf * qf, axis=1, keepdims=True) + 1e-06
            )
        c = s["g16"][pl.ds(4 * b, 4), :]
        beta = beta4[:, BLK * b : BLK * (b + 1)]
        rk4 = s["rows"][b, pl.ds(24, 4), :]
        end = c[:, BLK - 1 : BLK]
        ec = jnp.exp(c)
        s["rows"][b, pl.ds(0, 4), :] = c
        s["rows"][b, pl.ds(4, 4), :] = beta * rk4
        s["rows"][b, pl.ds(8, 4), :] = rk4 * jnp.exp(end - c)
        s["rows"][b, pl.ds(12, 4), :] = ec
        s["rows"][b, pl.ds(16, 4), :] = beta
        s["rows"][b, pl.ds(20, 4), :] = beta * rk4 * ec
        s["rows"][b, pl.ds(28, 4), :] = jnp.exp(jnp.broadcast_to(end, (4, BLK)))
        s["cols"][b] = s["rows"][b].T


def block_terms(kh, k_ref, q_ref, v_ref, s):
    row_ids = lax.broadcasted_iota(jnp.int32, (BLK, BLK), 0)
    col_ids = lax.broadcasted_iota(jnp.int32, (BLK, BLK), 1)
    inclusive = col_ids <= row_ids
    differ = row_ids ^ col_ids
    ident = jnp.where(row_ids == col_ids, 1.0, 0.0)
    key_lanes = slice(BLK * kh, BLK * (kh + 1))
    pairs = [(b, h) for b in range(NB) for h in (2 * kh, 2 * kh + 1)]
    for b in range(NB):
        tok = pl.ds(b * BLK, BLK)
        cols = s["cols"][b]
        kt = s["kt"][2 * b + kh]
        kk = dot(k_ref[tok, key_lanes], kt)
        qk = dot(q_ref[tok, key_lanes], kt)
        rk = s["rows"][b, pl.ds(24 + 2 * kh, 1), :]
        for h in (2 * kh, 2 * kh + 1):
            gap = cols[:, h : h + 1] - s["rows"][b, pl.ds(h, 1), :]
            ratio = jnp.exp(jnp.where(inclusive, gap, -1e30)) * rk
            s["mix"][4 * b + h] = (ratio * qk).astype(BF16)
            low = cols[:, 4 + h : 5 + h] * ratio * kk
            s["low"][2 * b + h % 2] = low
            s["inv"][2 * b + h % 2] = ident - jnp.where(differ == 1, low, 0.0)
        yield
    for level in range(1, 7):
        here = (differ >> level) == 1
        part = {}
        for b, h in pairs:
            n = 2 * b + h % 2
            off = jnp.where(here, s["low"][n], 0.0).astype(BF16)
            part[n] = dot(off, s["inv"][n].astype(BF16)).astype(BF16)
        yield
        for b, h in pairs:
            n = 2 * b + h % 2
            inv = s["inv"][n]
            s["inv"][n] = inv - dot(inv.astype(BF16), part[n])
        yield
    for b, h in pairs:
        tok = pl.ds(b * BLK, BLK)
        inv = s["inv"][2 * b + h % 2]
        t_v = (inv * s["rows"][b, pl.ds(16 + h, 1), :]).astype(BF16)
        t_k = (inv * s["rows"][b, pl.ds(20 + h, 1), :]).astype(BF16)
        s["upd"][4 * b + h] = dot(t_v, v_ref[tok, BLK * h : BLK * (h + 1)])
        s["wts"][4 * b + h] = dot(t_k, k_ref[tok, key_lanes]).astype(BF16)


def run_shard(kh, states, s):
    heads = (2 * kh, 2 * kh + 1)
    row_ids = lax.broadcasted_iota(jnp.int32, (BLK, 2 * BLK), 0)
    col_ids = lax.broadcasted_iota(jnp.int32, (BLK, 2 * BLK), 1)
    for h in heads:
        states[h] = jnp.where(row_ids + BLK == col_ids, 1.0, 0.0)
    for b in range(NB):
        cols = s["cols"][b]
        for h in heads:
            n = 4 * b + h
            state = states[h].astype(BF16)
            s["sb"][n] = state
            ws = dot(s["wts"][n], state)
            res_s = s["upd"][n] - ws[:, :BLK]
            res_a = -ws[:, BLK:]
            end = cols[:, 8 + h : 9 + h]
            s["rb"][n, :, :BLK] = res_s.astype(BF16)
            s["rb"][n, :, BLK:] = res_a.astype(BF16)
            s["re"][h, :, :BLK] = (end * res_s).astype(BF16)
            s["re"][h, :, BLK:] = (end * res_a).astype(BF16)
        yield
        for h in heads:
            gain = s["rows"][b, pl.ds(28 + h, 1), :]
            grow = dot(s["kt"][2 * b + kh], s["re"][h])
            states[h] = jnp.concatenate([gain, gain], axis=1) * states[h] + grow
        yield


def write_message(ref, c, fix, inject):
    c_ids = lax.broadcasted_iota(jnp.int32, (16, BLK), 0)
    hi, mid, low = (part.astype(F32) for part in split3(jnp.broadcast_to(c, (16, BLK))))
    terms = jnp.where(c_ids == 0, hi, jnp.where(c_ids == 1, mid, jnp.where(c_ids == 2, low, 0.0)))
    ref[:ROWS_D, :] = fix.astype(BF16)
    ref[ROWS_D:ROWS_C, :] = terms.astype(BF16)
    ref[ROWS_C:, :] = inject.astype(BF16)


def decay_of(ref):
    return jnp.sum(ref[ROWS_D:ROWS_C, :].astype(F32), axis=0, keepdims=True)


def compose(first, second, out):
    c_1, c_2 = decay_of(first), decay_of(second)
    prod = dot(first[...], second[:ROWS_D, :])
    fix = c_2 * first[:ROWS_D, :].astype(F32) + c_1 * second[:ROWS_D, :].astype(F32) - prod[:ROWS_D]
    inject = c_2 * first[ROWS_C:, :].astype(F32) + second[ROWS_C:, :].astype(F32) - prod[ROWS_C:]
    write_message(out, c_1 * c_2, fix, inject)


def step(ref, state):
    moved = decay_of(ref) * state - dot(state.astype(BF16), ref[:ROWS_D, :])
    return moved + ref[ROWS_C:, :].astype(F32)


def block_output(b, q_ref, s):
    tok = pl.ds(b * BLK, BLK)
    for h in range(NH):
        n = 4 * b + h
        kh = h // 2
        qs = dot(q_ref[tok, BLK * kh : BLK * (kh + 1)], s["sb"][n])
        out = s["cols"][b, :, 12 + h : 13 + h] * qs + dot(s["mix"][n], s["rb"][n])
        s["oloc"][h, tok, :] = out[:, :BLK]
        s["corr"][h, tok, :] = out[:, BLK:].astype(BF16)


def kernel(
    q_hbm, k_hbm, v_hbm, gl_hbm, bl_hbm, rate_hbm, gain_hbm, z_hbm, w_hbm, out_ref,
    q_ref, k_ref, v_ref, gl_ref, bl_ref, rate_ref, gain_ref, z_buf, w_buf,
    g16, rows, cols, rq, kt, mix, low, inv, upd, wts, sb, rb, re, msg, oloc, corr,
    gate, parts, rmsg, rowbuf, start, xst, xin,
    gated, parta, recva, partb, sumb, relay, hop, recvb,
    load_sem, m_send, m_recv, r_send, r_recv, x_send, x_recv,
    a_send, a_recv, f_send, f_recv, e_send, e_recv,
):
    s = dict(
        g16=g16, rows=rows, cols=cols, rq=rq, kt=kt, mix=mix, low=low, inv=inv, upd=upd, wts=wts,
        sb=sb, rb=rb, re=re, msg=msg, oloc=oloc, corr=corr,
    )
    loads = [
        pltpu.make_async_copy(src, dst, load_sem.at[i])
        for i, (src, dst) in enumerate([
            (gl_hbm, gl_ref), (bl_hbm, bl_ref), (rate_hbm, rate_ref), (k_hbm, k_ref), (q_hbm, q_ref),
            (v_hbm, v_ref), (gain_hbm, gain_ref), (z_hbm, z_buf), (w_hbm, w_buf),
        ])
    ]
    for load in loads:
        load.start()
    seq = lax.axis_index("seq")
    head = lax.axis_index("head")
    y, z = seq // NZ, seq % NZ
    x, core = head // 2, head % 2
    mine = z // 2
    owns = z % 2 == core

    def at(y_to, z_to):
        return (y_to * NZ + z_to, head)

    def owner(h):
        return at(y, 2 * h + core)

    def on_line(x_to, core_to):
        return (seq, 2 * x_to + core_to)

    def remote(src, dst, send, recv, device):
        return pltpu.make_async_remote_copy(
            src_ref=src, dst_ref=dst, send_sem=send, recv_sem=recv,
            device_id=device, device_id_type=pl.DeviceIdType.MESH,
        )

    ahead, behind = (x + 1) % NX, (x + NX - 1) % NX
    peers = [at(y, (z + i) % NZ) for i in range(1, NZ)]
    peers += [at((y + i) % NY, z) for i in range(1, NY)]
    peers += [on_line(ahead, core), on_line(behind, core), on_line(x, 1 - core)]
    barrier = pltpu.get_barrier_semaphore()
    for peer in peers:
        pl.semaphore_signal(barrier, inc=1, device_id=peer, device_id_type=pl.DeviceIdType.MESH)
    for load in loads[:6]:
        load.wait()

    gates(gl_ref, bl_ref, rate_ref, k_ref, q_ref, s)
    sends = []

    def go(copy):
        copy.start()
        sends.append(copy)

    row_ids = lax.broadcasted_iota(jnp.int32, (BLK, BLK), 0)
    eye = row_ids == lax.broadcasted_iota(jnp.int32, (BLK, BLK), 1)
    states = {}

    def send_heads(heads):
        for h in heads:
            total = g16[pl.ds(h, 1), :]
            for b in range(1, NB):
                total = total + g16[pl.ds(4 * b + h, 1), :]
            c = jnp.exp(jnp.broadcast_to(total[:, BLK - 1 : BLK], (1, BLK)))
            fix = jnp.where(eye, c, 0.0) - states[h][:, BLK:]
            write_message(msg.at[h], c, fix.T, states[h][:, :BLK].T)

            @pl.when(z != 2 * h + core)
            def _():
                remote(msg.at[h], parts.at[z], m_send.at[h], m_recv.at[z], owner(h)).start()

            @pl.when(z == 2 * h + core)
            def _():
                parts[z] = msg[h]

    for _ in block_terms(0, k_ref, q_ref, v_ref, s):
        pass
    second = block_terms(1, k_ref, q_ref, v_ref, s)
    for _ in run_shard(0, states, s):
        next(second)
    pl.semaphore_wait(barrier, len(peers))
    send_heads((0, 1))
    for _ in second:
        pass
    for _ in run_shard(1, states, s):
        pass
    send_heads((2, 3))
    for b in range(NB):
        block_output(b, q_ref, s)
    for load in loads[6:]:
        load.wait()
    zf = z_buf[...].astype(F32)
    zs = zf * sigmoid(zf)
    for h in range(NH):
        gate[:, BLK * h : BLK * (h + 1)] = zs[:, BLK * h : BLK * (h + 1)] * gain_ref[...]

    @pl.when(owns)
    def _():
        for k in range(4):
            for j in (2 * k, 2 * k + 1):

                @pl.when(z != j)
                def _():
                    remote(msg.at[0], parts.at[j], m_send.at[0], m_recv.at[j], at(y, z)).wait_recv()

            compose(parts.at[2 * k], parts.at[2 * k + 1], parts.at[8 + k])
        for k in range(2):
            compose(parts.at[8 + 2 * k], parts.at[9 + 2 * k], parts.at[12 + k])
        compose(parts.at[12], parts.at[13], rmsg)
        for i in range(NY - 1, 0, -1):

            @pl.when(y + i < NY)
            def _():
                remote(rmsg, rowbuf.at[y], r_send.at[i - 1], r_recv.at[y], at((y + i) % NY, z)).start()

        for first, second, out in PREFIXES:
            compose(parts.at[first], parts.at[second], parts.at[out])
        start[...] = jnp.zeros_like(start)
        for r in range(NY - 1):

            @pl.when(r < y)
            def _():
                remote(rmsg, rowbuf.at[r], r_send.at[0], r_recv.at[r], at(y, z)).wait_recv()
                if r == 0:
                    start[...] = rowbuf[r, ROWS_C:, :].astype(F32)
                else:
                    start[...] = step(rowbuf.at[r], start[...])

        row_state = start[...]
        for j, stretch in enumerate(BEFORE):
            at_shard = row_state if stretch is None else step(parts.at[stretch], row_state)
            xst[j] = at_shard.astype(BF16)

            @pl.when(j != z)
            def _():
                remote(xst.at[j], xin.at[mine], x_send.at[j], x_recv.at[mine], at(y, j)).start()

            @pl.when(j == z)
            def _():
                xin[mine] = xst[j]

    for h in range(NH):

        @pl.when(z != 2 * h + core)
        def _():
            remote(xst.at[0], xin.at[h], x_send.at[0], x_recv.at[h], at(y, z)).wait_recv()

    def gate_half(which, slot):
        toks = [pl.ds(pl.multiple_of((2 * j + which) * 64, 64), 64) for j in range(NX)]

        def rows_for(part):
            return jnp.concatenate([part(tok) for tok in toks], axis=0)

        for h in range(NH):
            lanes = slice(BLK * h, BLK * (h + 1))
            core_out = rows_for(lambda tok: oloc[h, tok, :])
            core_out = core_out + dot_nt(rows_for(lambda tok: corr[h, tok, :]), xin[h])
            r = rows_for(lambda tok: rq[h // 2, tok, :])
            mean = jnp.mean(core_out * core_out, axis=1, keepdims=True)
            scale = r * lax.rsqrt(r * r * mean + 1e-06)
            gated[slot, :, lanes] = (core_out * scale * rows_for(lambda tok: gate[tok, lanes])).astype(BF16)

    order = (0, 2, 1, 3)
    def send_over(n):
        parta[n] = dot(gated[0], w_buf[:, 512 * n : 512 * (n + 1)]).astype(BF16)
        go(remote(parta.at[n], recva.at[n], a_send.at[n], a_recv.at[n], on_line(x, 1 - core)))

    gate_half(1 - core, 0)
    send_over(order[0])
    gate_half(core, 1)

    def rows_of(chip):
        return pl.ds(pl.multiple_of(64 * chip, 64), 64)

    def ways(n):
        return (ahead, behind) if n < 2 else (behind, ahead)

    def send_on(n):
        onward, back = ways(n)
        remote(sumb.at[n, rows_of(x), :], relay.at[n], f_send.at[n], f_recv.at[n], on_line(x, core)).wait_recv()
        hop[n] = (partb[n, rows_of(onward), :] + relay[n].astype(F32)).astype(BF16)
        go(remote(hop.at[n], recvb.at[n, 1], e_send.at[n, 1], e_recv.at[n, 1], on_line(onward, core)))

    for count, n in enumerate(order):
        onward, back = ways(n)
        if count < 3:
            send_over(order[count + 1])
        partb[n] = dot(gated[1], w_buf[:, 512 * n : 512 * (n + 1)])
        remote(parta.at[n], recva.at[n], a_send.at[n], a_recv.at[n], on_line(x, core)).wait_recv()
        partb[n] = partb[n] + recva[n].astype(F32)
        sumb[n] = partb[n].astype(BF16)
        far = rows_of((x + 2) % NX)
        go(remote(sumb.at[n, far, :], relay.at[n], f_send.at[n], f_recv.at[n], on_line(onward, core)))
        go(remote(sumb.at[n, rows_of(back), :], recvb.at[n, 0], e_send.at[n, 0], e_recv.at[n, 0], on_line(back, core)))
        if count >= 2:
            send_on(order[count - 2])
    send_on(order[2])
    send_on(order[3])
    for n in order:
        total = partb[n, rows_of(x), :]
        for i in range(2):
            remote(
                hop.at[n], recvb.at[n, i], e_send.at[n, i], e_recv.at[n, i], on_line(x, core)
            ).wait_recv()
            total = total + recvb[n, i].astype(F32)
        out_ref[:, 512 * n : 512 * (n + 1)] = total.astype(BF16)

    for copy in sends:
        copy.wait_send()
    for h in range(NH):

        @pl.when(z != 2 * h + core)
        def _():
            remote(msg.at[h], parts.at[z], m_send.at[h], m_recv.at[z], owner(h)).wait_send()

    @pl.when(owns)
    def _():
        for j in range(NZ):

            @pl.when(j != z)
            def _():
                remote(xst.at[j], xin.at[mine], x_send.at[j], x_recv.at[mine], at(y, j)).wait_send()

        for i in range(1, NY):

            @pl.when(y + i < NY)
            def _():
                remote(rmsg, rowbuf.at[y], r_send.at[i - 1], r_recv.at[y], at((y + i) % NY, z)).wait_send()


def on_device(query, keys, values, gate_logit, beta_logit, decay_rate, norm_gain, gate_z, out_weight):
    hbm = pl.BlockSpec(memory_space=pltpu.HBM)
    dma = pltpu.SemaphoreType.DMA
    pairs = NB * NH
    scratch = [
        pltpu.VMEM((512, 256), BF16),
        pltpu.VMEM((512, 256), BF16),
        pltpu.VMEM((512, 512), BF16),
        pltpu.VMEM((NH, 512), F32),
        pltpu.VMEM((NH, 512), F32),
        pltpu.VMEM((1, NH), F32),
        pltpu.VMEM((1, BLK), F32),
        pltpu.VMEM((512, 512), BF16),
        pltpu.VMEM((512, 2048), BF16),
        pltpu.VMEM((16, BLK), F32),
        pltpu.VMEM((NB, 32, BLK), F32),
        pltpu.VMEM((NB, BLK, 32), F32),
        pltpu.VMEM((2, 512, 1), F32),
        pltpu.VMEM((2 * NB, BLK, BLK), BF16),
        pltpu.VMEM((pairs, BLK, BLK), BF16),
        pltpu.VMEM((8, BLK, BLK), F32),
        pltpu.VMEM((8, BLK, BLK), F32),
        pltpu.VMEM((pairs, BLK, BLK), F32),
        pltpu.VMEM((pairs, BLK, BLK), BF16),
        pltpu.VMEM((pairs, BLK, 2 * BLK), BF16),
        pltpu.VMEM((pairs, BLK, 2 * BLK), BF16),
        pltpu.VMEM((NH, BLK, 2 * BLK), BF16),
        pltpu.VMEM((NH, ROWS_M, BLK), BF16),
        pltpu.VMEM((NH, 512, BLK), F32),
        pltpu.VMEM((NH, 512, BLK), BF16),
        pltpu.VMEM((512, 512), F32),
        pltpu.VMEM((18, ROWS_M, BLK), BF16),
        pltpu.VMEM((ROWS_M, BLK), BF16),
        pltpu.VMEM((NY, ROWS_M, BLK), BF16),
        pltpu.VMEM((BLK, BLK), F32),
        pltpu.VMEM((NZ, BLK, BLK), BF16),
        pltpu.VMEM((NH, BLK, BLK), BF16),
        pltpu.VMEM((2, 256, 512), BF16),
        pltpu.VMEM((4, 256, 512), BF16),
        pltpu.VMEM((4, 256, 512), BF16),
        pltpu.VMEM((4, 256, 512), F32),
        pltpu.VMEM((4, 256, 512), BF16),
        pltpu.VMEM((4, 64, 512), BF16),
        pltpu.VMEM((4, 64, 512), BF16),
        pltpu.VMEM((4, 2, 64, 512), BF16),
        dma((9,)),
        dma((4,)), dma((8,)),
        dma((3,)), dma((4,)),
        dma((8,)), dma((4,)),
        dma((4,)), dma((4,)),
        dma((4,)), dma((4,)),
        dma((4, 2)), dma((4, 2)),
    ]
    return pl.pallas_call(
        kernel,
        out_shape=jax.ShapeDtypeStruct((64, 2048), BF16),
        in_specs=[hbm] * 9,
        out_specs=pl.BlockSpec(memory_space=pltpu.VMEM),
        scratch_shapes=scratch,
        compiler_params=pltpu.CompilerParams(
            collective_id=0, has_side_effects=True, vmem_limit_bytes=56 * 1024 * 1024
        ),
    )(
        query, keys, values, gate_logit.T, beta_logit.T, decay_rate.reshape(1, NH),
        norm_gain.reshape(1, BLK), gate_z, out_weight,
    )


def solution(mesh):
    return jax.shard_map(
        on_device,
        mesh=mesh,
        in_specs=(
            P("seq", "head"),
            P("seq", "head"),
            P("seq", "head"),
            P("seq", "head"),
            P("seq", "head"),
            P("head"),
            P(),
            P("seq", "head"),
            P("head", None),
        ),
        out_specs=P(("seq", "head"), None),
        check_vma=False,
    )
```
